32 devices in a mesh: tm: 2 (over y), rows: 4 (over z), dp: 4 (over x, core).
Axes of the slice: x: 2, y: 2, z: 4, core: 2. Of those that a mesh axis runs over, the one named last changes fastest.
Arguments:
- video: bfloat16 [4, 32, 16, 32, 128], P('dp', 'tm', 'rows'), may hold values from -6 to 6
- cotangent: bfloat16 [4, 32, 16, 32, 128], P('dp', 'tm', 'rows'), may hold values from -6 to 6
- in_kernel: bfloat16 [3, 3, 128, 128], replicated, may hold values from -0.03125 to 0.03125
- out_kernel: bfloat16 [3, 3, 128, 128], replicated, may hold values from -0.1875 to 0.1875
- skip_gain: float32 [128], replicated, may hold values from 0.5 to 1.5
- log_decay: float32 [32, 128], P('tm'), may hold values from -3 to 0, as said below
Outputs:
- layer_out: bfloat16 [4, 32, 16, 32, 128], P('dp', 'tm', 'rows')
- video_grad: bfloat16 [4, 32, 16, 32, 128], P('dp', 'tm', 'rows')
- in_kernel_grad: float32 [3, 3, 128, 128], replicated
- out_kernel_grad: float32 [3, 3, 128, 128], replicated
- skip_gain_grad: float32 [128], replicated
- decay_grad: float32 [32, 128], P('tm')
The draws below stay inside these ranges and needn't reach their ends.
Inputs may be any that keep to these rules, and one draw needn't show every extreme that they name: log_decay is negative.
All inputs are finite; a program needn't handle non-finite values.
Results may differ from the reference program's by a relative error of at most 0.0085.
Values may be sent and summed in bfloat16 or wider, within the bound.
No kernel may reach another device: no remote copies, remote signals or barrier semaphores. Data moves between devices by JAX's collectives and lax.ppermute only.
A program may use at most 64 MiB of HBM per device.

```python
import math
import jax
import jax.numpy as jnp
from jax import lax

U = 128
P_SIZE = 128
WIDTH = 32
FRAMES = 32
HEIGHT = 16
SEQS = 4


def draw_log_decay(key, part):
    keys = jax.random.split(jax.random.fold_in(key, 11), 6)
    share = 0.5
    slow = jax.random.uniform(keys[0], (P_SIZE,)) < share
    fast_rate = jnp.exp(jax.random.uniform(keys[1], (P_SIZE,), minval=math.log(0.045), maxval=math.log(0.08)))
    slow_rate = jnp.exp(jax.random.uniform(keys[2], (P_SIZE,), minval=math.log(0.1), maxval=math.log(1.0))) / FRAMES
    rate = jnp.where(slow, slow_rate, fast_rate)
    jitter = jnp.exp(jax.random.uniform(keys[3], (FRAMES, P_SIZE), minval=-0.5, maxval=0.5))
    base = -rate[None, :] * jitter
    spots = jax.random.randint(keys[4], (3,), 0, FRAMES)
    depth = jnp.log(jax.random.uniform(keys[5], (3, P_SIZE), minval=0.6, maxval=0.85))
    hits = (jnp.arange(FRAMES)[:, None] == spots[None, :]).astype(jnp.float32)
    return base + jnp.dot(hits, depth, precision=lax.Precision.HIGHEST)


def levels(key, extent, shards, low, largest):
    level, own = 1.0, jax.random.fold_in(key, 6)
    for dim, parts in shards:
        draws = jnp.exp(jax.random.uniform(jax.random.fold_in(own, dim), (parts,), jnp.float32, low / len(shards), largest / len(shards)))
        level = level * jnp.repeat(draws, extent[dim] // parts).reshape([-1 if axis == dim else 1 for axis in range(len(extent))])
    return level


def gaussian(own_key, extent, scale, most, cuts=(), held_as=jnp.bfloat16):
    drawn = scale * jax.random.normal(own_key, extent, jnp.float32)
    if cuts:
        drawn = drawn * levels(own_key, extent, cuts, -0.22, 0.18)
    return jnp.clip(drawn, -most, most).astype(held_as)


def setup_inputs(seed: int = 0) -> dict:
    key_of = jax.random.split(jax.random.key(seed), 7)
    return {
        "video": gaussian(key_of[0], (SEQS, FRAMES, HEIGHT, WIDTH, U), 1.0, 6.0, ((0, 4), (1, 2), (2, 4))),
        "cotangent": gaussian(key_of[1], (SEQS, FRAMES, HEIGHT, WIDTH, U), 1.0, 6.0, ((0, 4), (1, 2), (2, 4))),
        "in_kernel": gaussian(key_of[2], (3, 3, U, P_SIZE), (256 * U) ** -0.5, 0.03125),
        "out_kernel": gaussian(key_of[3], (3, 3, P_SIZE, U), (9 * P_SIZE) ** -0.5, 0.1875),
        "skip_gain": jnp.clip(jax.random.uniform(key_of[4], (U,), jnp.float32, 0.5, 1.5), 0.5, 1.5),
        "log_decay": draw_log_decay(jax.random.fold_in(key_of[6], 71), 0),
    }


def pad_both(field):
    return jnp.pad(field, ((0, 0), (0, 0), (1, 1), (1, 1), (0, 0)))

def forward_conv(padded, kernel):
    seqs, frames, rows_two, cols_two, chans = padded.shape
    rows, cols = (rows_two - 2, cols_two - 2)
    total = None
    for i in range(3):
        for j in range(3):
            piece = padded[:, :, i:i + rows, j:j + cols, :].reshape(-1, chans)
            term = jnp.dot(piece, kernel[i, j], preferred_element_type=jnp.float32)
            total = term if total is None else total + term
    return total.reshape(seqs, frames, rows, cols, kernel.shape[3])

def adjoint_conv(padded, kernel):
    seqs, frames, rows_two, cols_two, chans = padded.shape
    rows, cols = (rows_two - 2, cols_two - 2)
    total = None
    for i in range(3):
        for j in range(3):
            piece = padded[:, :, 2 - i:2 - i + rows, 2 - j:2 - j + cols, :].reshape(-1, chans)
            term = lax.dot_general(piece, kernel[i, j], (((1,), (1,)), ((), ())), preferred_element_type=jnp.float32)
            total = term if total is None else total + term
    return total.reshape(seqs, frames, rows, cols, kernel.shape[2])

def kernel_grad(padded, grad):
    seqs, frames, rows_two, cols_two, chans = padded.shape
    rows, cols = (rows_two - 2, cols_two - 2)
    flat_grad = grad.reshape(-1, grad.shape[-1])
    outer_list = []
    for i in range(3):
        inner_list = []
        for j in range(3):
            piece = padded[:, :, i:i + rows, j:j + cols, :].reshape(-1, chans)
            inner_list.append(lax.dot_general(piece, flat_grad, (((0,), (0,)), ((), ())), preferred_element_type=jnp.float32))
        outer_list.append(jnp.stack(inner_list))
    return jnp.stack(outer_list)

def reference(video, cotangent, in_kernel, out_kernel, skip_gain, log_decay):
    lam = jnp.exp(log_decay)

    def one_sequence(pair):
        frames_in, cot = pair
        padded_x = pad_both(frames_in)
        drive = forward_conv(padded_x, in_kernel)

        def forward_step(state, inputs):
            lam_t, drive_t = inputs
            state = lam_t * state + drive_t
            return (state, state)
        start = jnp.zeros(drive.shape[:1] + drive.shape[2:], jnp.float32)
        _, states = lax.scan(forward_step, start, (lam, jnp.moveaxis(drive, 1, 0)))
        states = jnp.moveaxis(states, 0, 1)
        states_bf = states.astype(jnp.bfloat16)
        padded_s = pad_both(states_bf)
        pre = forward_conv(padded_s, out_kernel) + skip_gain * frames_in.astype(jnp.float32)
        activated, pullback = jax.vjp(jax.nn.gelu, pre)
        grad_pre = pullback(cot.astype(jnp.float32))[0]
        grad_bf = grad_pre.astype(jnp.bfloat16)
        out_grad = kernel_grad(padded_s, grad_bf)
        gain_grad = lax.optimization_barrier(jnp.sum(grad_pre * frames_in.astype(jnp.float32), axis=(0, 1, 2, 3)))
        state_grad = adjoint_conv(pad_both(grad_bf), out_kernel)

        def back_step(carry, inputs):
            lam_t, grad_t = inputs
            adj = grad_t + carry
            return (lam_t * adj, adj)
        _, adjoint = lax.scan(back_step, start, (lam, jnp.moveaxis(state_grad, 1, 0)), reverse=True)
        adjoint = jnp.moveaxis(adjoint, 0, 1)
        previous = jnp.concatenate([jnp.zeros_like(states[:, :1]), states[:, :-1]], axis=1)
        decay_part = lax.optimization_barrier(jnp.sum(adjoint * lam[None, :, None, None, :] * previous, axis=(0, 2, 3)))
        adjoint_bf = adjoint.astype(jnp.bfloat16)
        in_grad = kernel_grad(padded_x, adjoint_bf)
        back = adjoint_conv(pad_both(adjoint_bf), in_kernel) + skip_gain * grad_pre
        return (activated.astype(jnp.bfloat16)[0], back.astype(jnp.bfloat16)[0], in_grad, out_grad, gain_grad, decay_part)
    outs = lax.map(one_sequence, (video[:, None], cotangent[:, None]))
    weight_scale = 1.0 / math.sqrt(SEQS * FRAMES * HEIGHT * WIDTH)
    decay_scale = 1.0 / math.sqrt(SEQS * HEIGHT * WIDTH)
    return (outs[0], outs[1], lax.optimization_barrier(jnp.sum(outs[2], axis=0)) * weight_scale, lax.optimization_barrier(jnp.sum(outs[3], axis=0)) * weight_scale, lax.optimization_barrier(jnp.sum(outs[4], axis=0)) * weight_scale, lax.optimization_barrier(jnp.sum(outs[5], axis=0)) * decay_scale)
```

```python
import functools
import math

import jax
import jax.numpy as jnp
from jax import lax
from jax.experimental import pallas as pl
from jax.experimental.pallas import tpu as pltpu
from jax.sharding import PartitionSpec as P

BF = jnp.bfloat16
F32 = jnp.float32
VMEM_LIMIT = 24 * 1024 * 1024
GELU_A = math.sqrt(2.0 / math.pi)
GELU_B = 0.044715


def vmem():
    return pl.BlockSpec(memory_space=pltpu.VMEM)


def smem():
    return pl.BlockSpec(memory_space=pltpu.SMEM)


def call(body, outs, ins, scalars, scratch=(), flops=0):
    moved = sum(math.prod(a.shape) * a.dtype.itemsize for a in list(ins) + list(outs))
    return pl.pallas_call(
        body,
        out_shape=outs,
        in_specs=[smem() if n < scalars else vmem() for n in range(len(ins))],
        out_specs=[vmem() for _ in outs],
        scratch_shapes=list(scratch),
        compiler_params=pltpu.CompilerParams(vmem_limit_bytes=VMEM_LIMIT),
        cost_estimate=pl.CostEstimate(flops=flops, bytes_accessed=moved, transcendentals=0),
    )(*ins)


def shape(dims, dtype):
    return jax.ShapeDtypeStruct(tuple(dims), dtype)


def columns(count, width, lanes):
    return lax.rem(lax.broadcasted_iota(jnp.int32, (count, lanes), 0), width)


def from_left(field, column):
    return jnp.where(column == 0, 0.0, pltpu.roll(field, 1, 0))


def from_right(field, column, width):
    return jnp.where(column == width - 1, 0.0, pltpu.roll(field, field.shape[0] - 1, 0))


def taps(field, first, rows):
    frames, _, cols, chans = field.shape
    return jnp.concatenate(
        [field[:, first + i : first + i + rows].reshape(frames * rows * cols, chans) for i in range(3)],
        axis=1,
    )


def conv(field, first, rows, weights):
    frames, _, cols, _ = field.shape
    out = weights.shape[1] // 3
    wide = jnp.dot(taps(field, first, rows), weights, preferred_element_type=F32)
    column = columns(wide.shape[0], cols, out)
    return (
        wide[:, out : 2 * out]
        + from_left(wide[:, :out], column)
        + from_right(wide[:, 2 * out :], column, cols)
    )


def spread(grad, cols):
    column = columns(grad.shape[0], cols, grad.shape[1])
    return jnp.concatenate(
        [
            from_right(grad, column, cols).astype(BF),
            grad.astype(BF),
            from_left(grad, column).astype(BF),
        ],
        axis=1,
    )


def outer(left, right):
    return lax.dot_general(left, right, (((0,), (0,)), ((), ())), preferred_element_type=F32)


def group_of(frames, most):
    size = most
    while frames % size:
        size -= 1
    return size


def fill_halo(edge_ref, wide_ref, own_ref, first_ref, second_ref):
    rows, deep = own_ref.shape[1], first_ref.shape[1]
    odd = edge_ref[2] == 1
    wide_ref[:, deep : deep + rows] = own_ref[...]
    wide_ref[:, pl.ds(jnp.where(odd, 0, rows + deep), deep)] = first_ref[...]
    wide_ref[:, pl.ds(jnp.where(odd, rows + deep, 0), deep)] = second_ref[...]


def inside(edge_ref, field, width):
    count = field.shape[0]
    upper = jnp.where(edge_ref[0] == 1, field[:width], 0.0)
    lower = jnp.where(edge_ref[1] == 1, field[count - width :], 0.0)
    return jnp.concatenate([upper, field[width : count - width], lower], axis=0)


def drive_kernel(edge_ref, own_ref, first_ref, second_ref, kernel_ref, lam_ref, wide_ref, local_ref, end_ref):
    frames, rows, cols, _ = own_ref.shape
    state_chans = kernel_ref.shape[1] // 3
    fill_halo(edge_ref, wide_ref, own_ref, first_ref, second_ref)
    group = group_of(frames, 2)
    many = (rows + 2) * cols

    def step(n, state):
        base = n * group
        drive = conv(wide_ref[pl.ds(base, group)], 0, rows + 2, kernel_ref[...])
        for k in range(group):
            now = inside(edge_ref, drive[k * many : (k + 1) * many], cols)
            state = lam_ref[base + k] * state + now
            local_ref[base + k] = state.reshape(rows + 2, cols, state_chans)
        return state

    last = lax.fori_loop(0, frames // group, step, jnp.zeros((many, state_chans), F32))
    end_ref[...] = last.reshape(rows + 2, cols, state_chans).astype(BF)


def layer_kernel(
    local_ref, carry_ref, reach_ref, own_ref, cot_ref, kernel_ref, gain_ref,
    state_ref, act_ref, grad_ref, gain_grad_ref,
):
    frames, rows, cols, chans = own_ref.shape
    group = group_of(frames, 2)
    many = group * rows * cols
    carry = carry_ref[...].astype(F32)

    def step(n, total):
        base = n * group
        state = jnp.stack(
            [(local_ref[base + k] + reach_ref[base + k] * carry).astype(BF) for k in range(group)]
        )
        state_ref[pl.ds(base, group)] = state
        own = own_ref[pl.ds(base, group)].reshape(many, chans).astype(F32)
        pre = conv(state, 0, rows, kernel_ref[...]) + gain_ref[...] * own
        square = pre * pre
        bend = jnp.tanh(GELU_A * (pre + GELU_B * square * pre))
        half = 0.5 * (1.0 + bend)
        slope = half + 0.5 * pre * (1.0 - bend * bend) * (GELU_A * (1.0 + 3.0 * GELU_B * square))
        grad = cot_ref[pl.ds(base, group)].reshape(many, chans).astype(F32) * slope
        act_ref[pl.ds(base, group)] = (pre * half).astype(BF).reshape(group, rows, cols, chans)
        grad_ref[pl.ds(base, group)] = grad.astype(BF).reshape(group, rows, cols, chans)
        return total + jnp.sum((grad * own).reshape(many // 8, 8, chans), axis=0)

    total = lax.fori_loop(0, frames // group, step, jnp.zeros((8, chans), F32))
    gain_grad_ref[...] = jnp.sum(total, axis=0, keepdims=True)


def put_blocks(total, out_ref, scale):
    left, right = out_ref.shape[2:]
    for i in range(3):
        for j in range(3):
            out_ref[i, j] = (
                total[i * left : (i + 1) * left, j * right : (j + 1) * right] * scale
            ).astype(out_ref.dtype)


def out_grad_kernel(scale, state_ref, grad_ref, out_ref, total_ref):
    frames, rows, cols, chans = grad_ref.shape
    group = group_of(frames, 4)
    total_ref[...] = jnp.zeros_like(total_ref)

    def step(n, _):
        base = n * group
        grad = grad_ref[pl.ds(base, group)].reshape(group * rows * cols, chans).astype(F32)
        left = taps(state_ref[pl.ds(base, group)], 0, rows)
        total_ref[...] += outer(left, spread(grad, cols))
        return 0

    lax.fori_loop(0, frames // group, step, 0)
    put_blocks(total_ref[...], out_ref, scale)


def back_kernel(edge_ref, own_ref, first_ref, second_ref, kernel_ref, lam_ref, local_ref, lead_ref, wide_ref):
    frames, rows, cols, _ = own_ref.shape
    state_chans = kernel_ref.shape[1] // 3
    fill_halo(edge_ref, wide_ref, own_ref, first_ref, second_ref)
    group = group_of(frames, 2)
    many = (rows + 2) * cols

    def step(n, carry):
        base = frames - (n + 1) * group
        flow = conv(wide_ref[pl.ds(base, group)], 0, rows + 2, kernel_ref[...])
        for k in reversed(range(group)):
            adjoint = inside(edge_ref, flow[k * many : (k + 1) * many], cols) + carry
            local_ref[base + k] = adjoint.reshape(rows + 2, cols, state_chans)
            carry = lam_ref[base + k] * adjoint
        return carry

    lead = lax.fori_loop(0, frames // group, step, jnp.zeros((many, state_chans), F32))
    lead_ref[...] = lead.reshape(rows + 2, cols, state_chans).astype(BF)


def in_grad_kernel(
    scale, decay_scale, local_ref, back_ref, reach_ref, lam_ref, wide_ref, state_ref, carry_ref,
    adjoint_ref, out_ref, decay_ref, total_ref,
):
    frames, rows_two, cols, chans = local_ref.shape
    rows = rows_two - 2
    group = group_of(frames, 4)
    many = rows * cols
    back = back_ref[...].astype(F32)
    total_ref[...] = jnp.zeros_like(total_ref)

    def step(n, previous):
        base = n * group
        kept = []
        for k in range(group):
            adjoint = local_ref[base + k] + reach_ref[base + k] * back
            adjoint_ref[base + k] = adjoint.astype(BF)
            mine = adjoint[1 : 1 + rows].reshape(many, chans)
            kept.append(mine)
            part = jnp.sum((mine * previous).reshape(many // 8, 8, chans), axis=0)
            decay_ref[base + k] = jnp.sum(part, axis=0, keepdims=True) * lam_ref[base + k] * decay_scale
            previous = state_ref[base + k, 1 : 1 + rows].reshape(many, chans).astype(F32)
        left = taps(wide_ref[pl.ds(base, group)], 1, rows)
        total_ref[...] += outer(left, spread(jnp.concatenate(kept, axis=0), cols))
        return previous

    before = carry_ref[1 : 1 + rows].reshape(many, chans).astype(F32)
    lax.fori_loop(0, frames // group, step, before)
    put_blocks(total_ref[...], out_ref, scale)


def video_grad_kernel(adjoint_ref, grad_ref, kernel_ref, gain_ref, out_ref):
    frames, rows, cols, chans = grad_ref.shape
    group = group_of(frames, 2)

    def step(n, _):
        base = n * group
        grad = grad_ref[pl.ds(base, group)].reshape(group * rows * cols, chans).astype(F32)
        flow = conv(adjoint_ref[pl.ds(base, group)], 0, rows, kernel_ref[...])
        out_ref[pl.ds(base, group)] = (
            (flow + gain_ref[...] * grad).astype(BF).reshape(group, rows, cols, chans)
        )
        return 0

    lax.fori_loop(0, frames // group, step, 0)


def halo_pair(field, deep):
    count = lax.axis_size("rows")
    odd = lax.rem(lax.axis_index("rows"), 2)
    rows = field.shape[1]
    swap = lambda low: [p for i in range(low, count - 1, 2) for p in ((i, i + 1), (i + 1, i))]
    pick = lambda flag: lax.dynamic_slice_in_dim(field, flag * (rows - deep), deep, axis=1)
    first, second = pick(1 - odd), pick(odd)
    return lax.ppermute(first, "rows", swap(0)), lax.ppermute(second, "rows", swap(1))


def from_earlier(end, totals):
    count = lax.axis_size("tm")
    found, between = None, None
    for k in range(1, count):
        pairs = [(i, i + k) for i in range(count - k)]
        piece = lax.ppermute(end, "tm", pairs)
        if k == 1:
            found = piece.astype(F32)
        else:
            step = lax.ppermute(totals, "tm", [(i, i + k - 1) for i in range(count - k + 1)])
            between = step if between is None else between + step
            found = found + jnp.exp(between) * piece.astype(F32)
    if found is None:
        return jnp.zeros(end.shape, BF)
    return found.astype(BF)


def from_later(lead, totals):
    count = lax.axis_size("tm")
    found, between = None, None
    for k in range(1, count):
        pairs = [(i + k, i) for i in range(count - k)]
        piece = lax.ppermute(lead, "tm", pairs)
        if k == 1:
            found = piece.astype(F32)
        else:
            step = lax.ppermute(totals, "tm", [(i + k - 1, i) for i in range(count - k + 1)])
            between = step if between is None else between + step
            found = found + jnp.exp(between) * piece.astype(F32)
    if found is None:
        return jnp.zeros(lead.shape, BF)
    return found.astype(BF)


def tree_sum(part):
    stages = []
    for axis in ("dp", "tm", "rows"):
        size, mask = lax.axis_size(axis), 1
        while mask < size:
            stages.append((axis, mask))
            mask *= 2
    split = 2 if part.shape[0] % 64 == 0 else 0
    swap = lambda value, axis, mask: lax.ppermute(
        value, axis, [(i, i ^ mask) for i in range(lax.axis_size(axis))]
    )
    bit = lambda axis, mask: jnp.where((lax.axis_index(axis) & mask) != 0, 1, 0)
    done = []
    for axis, mask in stages[:split]:
        half = part.shape[0] // 2
        mine = bit(axis, mask)
        sent = lax.dynamic_slice_in_dim(part, (1 - mine) * half, half, axis=0).astype(BF)
        kept = lax.dynamic_slice_in_dim(part, mine * half, half, axis=0)
        part = kept.astype(F32) + swap(sent, axis, mask).astype(F32)
        done.append((axis, mask))
    whole = part.astype(BF)
    for axis, mask in stages[split:]:
        whole = (whole.astype(F32) + swap(whole, axis, mask).astype(F32)).astype(BF)
    for axis, mask in reversed(done):
        other = swap(whole, axis, mask)
        mine = bit(axis, mask) == 1
        whole = jnp.where(
            mine, jnp.concatenate([other, whole], axis=0), jnp.concatenate([whole, other], axis=0)
        )
    return whole


def on_device(video, cotangent, in_kernel, out_kernel, skip_gain, log_decay):
    seqs, frames, rows, cols, chans = video.shape
    state_chans = in_kernel.shape[3]
    sizes = {axis: lax.axis_size(axis) for axis in ("tm", "rows", "dp")}
    devices = sizes["tm"] * sizes["rows"] * sizes["dp"]
    for size in sizes.values():
        assert size & (size - 1) == 0
    assert seqs == 1 and rows >= 2
    video, cotangent = video[0], cotangent[0]
    band = lax.axis_index("rows")
    edge = jnp.stack(
        [jnp.where(band > 0, 1, 0), jnp.where(band < sizes["rows"] - 1, 1, 0), lax.rem(band, 2)]
    ).astype(jnp.int32)
    cum = jnp.cumsum(log_decay, axis=0)
    totals = cum[-1:]
    lam = jnp.exp(log_decay)[:, None, :]
    reach = jnp.exp(cum)[:, None, :]
    back_reach = jnp.exp(totals - cum)[:, None, :]
    gain = skip_gain[None, :]
    flat = lambda k: k.transpose(0, 2, 1, 3).reshape(3 * k.shape[2], 3 * k.shape[3])
    flip = lambda k: k[::-1, ::-1].transpose(0, 3, 1, 2).reshape(3 * k.shape[3], 3 * k.shape[2])
    wide_rows = frames * (rows + 2) * cols
    narrow_rows = frames * rows * cols
    each = 2 * 9 * chans * state_chans
    weight_scale = 1.0 / math.sqrt(devices * narrow_rows * seqs)
    decay_scale = 1.0 / math.sqrt(seqs * rows * cols * sizes["rows"] * sizes["dp"])

    first, second = halo_pair(video, 2)
    wide, local, end = call(
        drive_kernel,
        [
            shape((frames, rows + 4, cols, chans), BF),
            shape((frames, rows + 2, cols, state_chans), F32),
            shape((rows + 2, cols, state_chans), BF),
        ],
        [edge, video, first, second, flat(in_kernel), lam],
        1,
        flops=each * wide_rows,
    )
    carry = from_earlier(end, totals)
    state, act, grad, gain_part = call(
        layer_kernel,
        [
            shape((frames, rows + 2, cols, state_chans), BF),
            shape(video.shape, BF),
            shape(video.shape, BF),
            shape((1, chans), F32),
        ],
        [local, carry, reach, video, cotangent, flat(out_kernel), gain],
        0,
        flops=each * narrow_rows,
    )
    first, second = halo_pair(grad, 2)
    (out_part,) = call(
        functools.partial(out_grad_kernel, weight_scale),
        [shape((3, 3, state_chans, chans), F32)],
        [state, grad],
        0,
        scratch=[pltpu.VMEM((3 * state_chans, 3 * chans), F32)],
        flops=each * narrow_rows,
    )
    local, lead = call(
        back_kernel,
        [
            shape((frames, rows + 2, cols, state_chans), F32),
            shape((rows + 2, cols, state_chans), BF),
        ],
        [edge, grad, first, second, flip(out_kernel), lam],
        1,
        scratch=[pltpu.VMEM((frames, rows + 4, cols, chans), BF)],
        flops=each * wide_rows,
    )
    back = from_later(lead, totals)
    adjoint, in_part, decay_part = call(
        functools.partial(in_grad_kernel, weight_scale, decay_scale),
        [
            shape((frames, rows + 2, cols, state_chans), BF),
            shape((3, 3, chans, state_chans), F32),
            shape((frames, 1, state_chans), F32),
        ],
        [local, back, back_reach, lam, wide, state, carry],
        0,
        scratch=[pltpu.VMEM((3 * chans, 3 * state_chans), F32)],
        flops=each * narrow_rows,
    )
    (video_grad,) = call(
        video_grad_kernel,
        [shape(video.shape, BF)],
        [adjoint, grad, flip(in_kernel), gain],
        0,
        flops=each * narrow_rows,
    )
    block = lax.axis_index("tm")
    slots = jnp.where(
        jnp.arange(sizes["tm"])[:, None, None] == block, decay_part[:, 0][None], 0.0
    ).reshape(-1, state_chans)
    pieces = [
        in_part.reshape(-1, state_chans),
        out_part.reshape(-1, chans),
        slots,
        gain_part * weight_scale,
    ]
    used = sum(p.shape[0] for p in pieces)
    pieces.append(jnp.zeros((-used % 64, chans), F32))
    total = tree_sum(jnp.concatenate(pieces, axis=0)).astype(F32)
    at = 0
    sums = []
    for piece in pieces[:4]:
        sums.append(lax.slice_in_dim(total, at, at + piece.shape[0], axis=0))
        at += piece.shape[0]
    return (
        act[None],
        video_grad[None],
        sums[0].reshape(3, 3, chans, state_chans),
        sums[1].reshape(3, 3, state_chans, chans),
        sums[3][0],
        lax.dynamic_slice_in_dim(sums[2], block * frames, frames, axis=0),
    )


def solution(mesh):
    placed = (
        P("dp", "tm", "rows", None, None),
        P("dp", "tm", "rows", None, None),
        P(),
        P(),
        P(),
        P("tm", None),
    )
    return jax.shard_map(
        on_device,
        mesh=mesh,
        in_specs=placed,
        out_specs=(
            P("dp", "tm", "rows", None, None),
            P("dp", "tm", "rows", None, None),
            P(),
            P(),
            P(),
            P("tm", None),
        ),
        check_vma=False,
    )
```

```python
import functools
import math

import jax
import jax.numpy as jnp
from jax import lax
from jax.experimental import pallas as pl
from jax.experimental.pallas import tpu as pltpu
from jax.sharding import PartitionSpec as P

BF = jnp.bfloat16
F32 = jnp.float32
VMEM_LIMIT = 24 * 1024 * 1024
GELU_A = math.sqrt(2.0 / math.pi)
GELU_B = 0.044715


def vmem():
    return pl.BlockSpec(memory_space=pltpu.VMEM)


def smem():
    return pl.BlockSpec(memory_space=pltpu.SMEM)


def call(body, outs, ins, scalars, scratch=(), flops=0):
    moved = sum(math.prod(a.shape) * a.dtype.itemsize for a in list(ins) + list(outs))
    return pl.pallas_call(
        body,
        out_shape=outs,
        in_specs=[smem() if n < scalars else vmem() for n in range(len(ins))],
        out_specs=[vmem() for _ in outs],
        scratch_shapes=list(scratch),
        compiler_params=pltpu.CompilerParams(vmem_limit_bytes=VMEM_LIMIT),
        cost_estimate=pl.CostEstimate(flops=flops, bytes_accessed=moved, transcendentals=0),
    )(*ins)


def shape(dims, dtype):
    return jax.ShapeDtypeStruct(tuple(dims), dtype)


def columns(count, width, lanes):
    return lax.rem(lax.broadcasted_iota(jnp.int32, (count, lanes), 0), width)


def from_left(field, column):
    return jnp.where(column == 0, 0.0, pltpu.roll(field, 1, 0))


def from_right(field, column, width):
    return jnp.where(column == width - 1, 0.0, pltpu.roll(field, field.shape[0] - 1, 0))


def taps(field, first, rows):
    frames, _, cols, chans = field.shape
    return jnp.concatenate(
        [field[:, first + i : first + i + rows].reshape(frames * rows * cols, chans) for i in range(3)],
        axis=1,
    )


def conv(field, first, rows, weights):
    _, _, cols, _ = field.shape
    out = weights.shape[1] // 3
    wide = jnp.dot(taps(field, first, rows), weights, preferred_element_type=F32)
    column = columns(wide.shape[0], cols, out)
    return (
        wide[:, out : 2 * out]
        + from_left(wide[:, :out], column)
        + from_right(wide[:, 2 * out :], column, cols)
    )


def spread(grad, cols):
    column = columns(grad.shape[0], cols, grad.shape[1])
    return jnp.concatenate(
        [
            from_right(grad, column, cols).astype(BF),
            grad.astype(BF),
            from_left(grad, column).astype(BF),
        ],
        axis=1,
    )


def outer(left, right):
    return lax.dot_general(left, right, (((0,), (0,)), ((), ())), preferred_element_type=F32)


def group_of(frames, most):
    size = most
    while frames % size:
        size -= 1
    return size


def fill_halo(edge_ref, wide_ref, own_ref, first_ref, second_ref):
    rows, deep = own_ref.shape[1], first_ref.shape[1]
    odd = edge_ref[2] == 1
    wide_ref[:, deep : deep + rows] = own_ref[...]
    wide_ref[:, pl.ds(jnp.where(odd, 0, rows + deep), deep)] = first_ref[...]
    wide_ref[:, pl.ds(jnp.where(odd, rows + deep, 0), deep)] = second_ref[...]


def inside(edge_ref, field, width):
    count = field.shape[0]
    upper = jnp.where(edge_ref[0] == 1, field[:width], 0.0)
    lower = jnp.where(edge_ref[1] == 1, field[count - width :], 0.0)
    return jnp.concatenate([upper, field[width : count - width], lower], axis=0)


def drive_kernel(edge_ref, own_ref, first_ref, second_ref, kernel_ref, lam_ref, wide_ref, local_ref, end_ref):
    frames, rows, cols, _ = own_ref.shape
    state_chans = kernel_ref.shape[1] // 3
    fill_halo(edge_ref, wide_ref, own_ref, first_ref, second_ref)
    group = group_of(frames, 16)
    many = (rows + 2) * cols

    def step(n, state):
        base = n * group
        drive = conv(wide_ref[pl.ds(base, group)], 0, rows + 2, kernel_ref[...])
        for k in range(group):
            now = inside(edge_ref, drive[k * many : (k + 1) * many], cols)
            state = lam_ref[base + k] * state + now
            local_ref[base + k] = state.reshape(rows + 2, cols, state_chans)
        return state

    last = lax.fori_loop(0, frames // group, step, jnp.zeros((many, state_chans), F32))
    end_ref[...] = last.reshape(rows + 2, cols, state_chans).astype(BF)


def layer_kernel(
    local_ref, carry_ref, reach_ref, own_ref, cot_ref, kernel_ref, gain_ref,
    state_ref, act_ref, grad_ref, gain_grad_ref,
):
    frames, rows, cols, chans = own_ref.shape
    group = group_of(frames, 16)
    many = group * rows * cols
    carry = carry_ref[...].astype(F32)

    def step(n, total):
        base = n * group
        state = jnp.stack(
            [(local_ref[base + k] + reach_ref[base + k] * carry).astype(BF) for k in range(group)]
        )
        state_ref[pl.ds(base, group)] = state
        own = own_ref[pl.ds(base, group)].reshape(many, chans).astype(F32)
        pre = conv(state, 0, rows, kernel_ref[...]) + gain_ref[...] * own
        square = pre * pre
        bend = jnp.tanh(GELU_A * (pre + GELU_B * square * pre))
        half = 0.5 * (1.0 + bend)
        slope = half + 0.5 * pre * (1.0 - bend * bend) * (GELU_A * (1.0 + 3.0 * GELU_B * square))
        grad = cot_ref[pl.ds(base, group)].reshape(many, chans).astype(F32) * slope
        act_ref[pl.ds(base, group)] = (pre * half).astype(BF).reshape(group, rows, cols, chans)
        grad_ref[pl.ds(base, group)] = grad.astype(BF).reshape(group, rows, cols, chans)
        return total + jnp.sum((grad * own).reshape(many // 8, 8, chans), axis=0)

    total = lax.fori_loop(0, frames // group, step, jnp.zeros((8, chans), F32))
    gain_grad_ref[...] = jnp.sum(total, axis=0, keepdims=True)


def put_blocks(total, out_ref, scale):
    left, right = out_ref.shape[2:]
    for i in range(3):
        for j in range(3):
            out_ref[i, j] = (
                total[i * left : (i + 1) * left, j * right : (j + 1) * right] * scale
            ).astype(out_ref.dtype)


def out_grad_kernel(scale, state_ref, grad_ref, out_ref, total_ref):
    frames, rows, cols, chans = grad_ref.shape
    group = group_of(frames, 16)
    total_ref[...] = jnp.zeros_like(total_ref)

    def step(n, _):
        base = n * group
        grad = grad_ref[pl.ds(base, group)].reshape(group * rows * cols, chans).astype(F32)
        left = taps(state_ref[pl.ds(base, group)], 0, rows)
        total_ref[...] += outer(left, spread(grad, cols))
        return 0

    lax.fori_loop(0, frames // group, step, 0)
    put_blocks(total_ref[...], out_ref, scale)


def back_kernel(edge_ref, own_ref, first_ref, second_ref, kernel_ref, lam_ref, local_ref, lead_ref, wide_ref):
    frames, rows, cols, _ = own_ref.shape
    state_chans = kernel_ref.shape[1] // 3
    fill_halo(edge_ref, wide_ref, own_ref, first_ref, second_ref)
    group = group_of(frames, 16)
    many = (rows + 2) * cols

    def step(n, carry):
        base = frames - (n + 1) * group
        flow = conv(wide_ref[pl.ds(base, group)], 0, rows + 2, kernel_ref[...])
        for k in reversed(range(group)):
            adjoint = inside(edge_ref, flow[k * many : (k + 1) * many], cols) + carry
            local_ref[base + k] = adjoint.reshape(rows + 2, cols, state_chans)
            carry = lam_ref[base + k] * adjoint
        return carry

    lead = lax.fori_loop(0, frames // group, step, jnp.zeros((many, state_chans), F32))
    lead_ref[...] = lead.reshape(rows + 2, cols, state_chans).astype(BF)


def in_grad_kernel(
    scale, decay_scale, local_ref, back_ref, reach_ref, lam_ref, wide_ref, state_ref, carry_ref,
    adjoint_ref, out_ref, decay_ref, total_ref,
):
    frames, rows_two, cols, chans = local_ref.shape
    rows = rows_two - 2
    group = group_of(frames, 16)
    many = rows * cols
    back = back_ref[...].astype(F32)
    total_ref[...] = jnp.zeros_like(total_ref)

    def step(n, previous):
        base = n * group
        kept = []
        for k in range(group):
            adjoint = local_ref[base + k] + reach_ref[base + k] * back
            adjoint_ref[base + k] = adjoint.astype(BF)
            mine = adjoint[1 : 1 + rows].reshape(many, chans)
            kept.append(mine)
            part = jnp.sum((mine * previous).reshape(many // 8, 8, chans), axis=0)
            decay_ref[base + k] = jnp.sum(part, axis=0, keepdims=True) * lam_ref[base + k] * decay_scale
            previous = state_ref[base + k, 1 : 1 + rows].reshape(many, chans).astype(F32)
        left = taps(wide_ref[pl.ds(base, group)], 1, rows)
        total_ref[...] += outer(left, spread(jnp.concatenate(kept, axis=0), cols))
        return previous

    before = carry_ref[1 : 1 + rows].reshape(many, chans).astype(F32)
    lax.fori_loop(0, frames // group, step, before)
    put_blocks(total_ref[...], out_ref, scale)


def video_grad_kernel(adjoint_ref, grad_ref, kernel_ref, gain_ref, out_ref):
    frames, rows, cols, chans = grad_ref.shape
    group = group_of(frames, 16)

    def step(n, _):
        base = n * group
        grad = grad_ref[pl.ds(base, group)].reshape(group * rows * cols, chans).astype(F32)
        flow = conv(adjoint_ref[pl.ds(base, group)], 0, rows, kernel_ref[...])
        out_ref[pl.ds(base, group)] = (
            (flow + gain_ref[...] * grad).astype(BF).reshape(group, rows, cols, chans)
        )
        return 0

    lax.fori_loop(0, frames // group, step, 0)


def halo_pair(field, deep):
    count = lax.axis_size("rows")
    odd = lax.rem(lax.axis_index("rows"), 2)
    rows = field.shape[1]
    swap = lambda low: [p for i in range(low, count - 1, 2) for p in ((i, i + 1), (i + 1, i))]
    pick = lambda flag: lax.dynamic_slice_in_dim(field, flag * (rows - deep), deep, axis=1)
    first, second = pick(1 - odd), pick(odd)
    return lax.ppermute(first, "rows", swap(0)), lax.ppermute(second, "rows", swap(1))


def from_earlier(end, totals):
    count = lax.axis_size("tm")
    found, between = None, None
    for k in range(1, count):
        pairs = [(i, i + k) for i in range(count - k)]
        piece = lax.ppermute(end, "tm", pairs)
        if k == 1:
            found = piece.astype(F32)
        else:
            step = lax.ppermute(totals, "tm", [(i, i + k - 1) for i in range(count - k + 1)])
            between = step if between is None else between + step
            found = found + jnp.exp(between) * piece.astype(F32)
    if found is None:
        return jnp.zeros(end.shape, BF)
    return found.astype(BF)


def from_later(lead, totals):
    count = lax.axis_size("tm")
    found, between = None, None
    for k in range(1, count):
        pairs = [(i + k, i) for i in range(count - k)]
        piece = lax.ppermute(lead, "tm", pairs)
        if k == 1:
            found = piece.astype(F32)
        else:
            step = lax.ppermute(totals, "tm", [(i + k - 1, i) for i in range(count - k + 1)])
            between = step if between is None else between + step
            found = found + jnp.exp(between) * piece.astype(F32)
    if found is None:
        return jnp.zeros(lead.shape, BF)
    return found.astype(BF)


def tree_sum(part):
    axes = ("tm", "rows", "dp")
    bits, scale = [], 1
    for axis in reversed(axes):
        size = 1
        while size < lax.axis_size(axis):
            bits.append((axis, size, size * scale))
            size *= 2
        scale *= lax.axis_size(axis)
    near = [b for b in bits if b[0] == "dp"][:2] + [b for b in bits if b[0] == "tm"][:1]
    far = [b for b in bits if b not in near]
    devices = scale

    def swap(value, mask):
        return lax.ppermute(value, axes, [(i, i ^ mask) for i in range(devices)])

    def place(group):
        spot = 0
        for n, (axis, mask, _) in enumerate(group):
            spot = spot + jnp.where((lax.axis_index(axis) & mask) != 0, 1 << n, 0)
        return spot

    def combined(group, k):
        return sum(mask for n, (_, _, mask) in enumerate(group) if (k >> n) & 1)

    done = []
    for stage, group in enumerate((near[:1], near[1:])):
        if not group:
            continue
        ways = 1 << len(group)
        size = part.shape[0] // ways
        spot = place(group)
        chunk = lambda k: lax.dynamic_slice_in_dim(part, (spot ^ k) * size, size, axis=0)
        sent = [chunk(k).astype(BF) for k in range(1, ways)]
        found = [swap(v, combined(group, k + 1)) for k, v in enumerate(sent)]
        part = chunk(0)
        for piece in found:
            part = part + piece.astype(F32)
        done.append((stage, group, spot))
    whole = part.astype(BF)
    for _, _, mask in far:
        whole = (whole.astype(F32) + swap(whole, mask).astype(F32)).astype(BF)
    for stage, group, spot in reversed(done):
        ways, size = 1 << len(group), whole.shape[0]
        found = [swap(whole, combined(group, k)) for k in range(1, ways)]
        joined = jnp.zeros((ways * size, whole.shape[1]), BF)
        for k, piece in enumerate([whole, *found]):
            joined = lax.dynamic_update_slice_in_dim(joined, piece, (spot ^ k) * size, axis=0)
        whole = joined
    return whole


def on_device(video, cotangent, in_kernel, out_kernel, skip_gain, log_decay):
    seqs, frames, rows, cols, chans = video.shape
    state_chans = in_kernel.shape[3]
    sizes = {axis: lax.axis_size(axis) for axis in ("tm", "rows", "dp")}
    devices = sizes["tm"] * sizes["rows"] * sizes["dp"]
    for size in sizes.values():
        assert size & (size - 1) == 0
    assert seqs == 1 and rows >= 2
    video, cotangent = video[0], cotangent[0]
    band = lax.axis_index("rows")
    edge = jnp.stack(
        [jnp.where(band > 0, 1, 0), jnp.where(band < sizes["rows"] - 1, 1, 0), lax.rem(band, 2)]
    ).astype(jnp.int32)
    cum = jnp.cumsum(log_decay, axis=0)
    totals = cum[-1:]
    lam = jnp.exp(log_decay)[:, None, :]
    reach = jnp.exp(cum)[:, None, :]
    back_reach = jnp.exp(totals - cum)[:, None, :]
    gain = skip_gain[None, :]
    flat = lambda k: k.transpose(0, 2, 1, 3).reshape(3 * k.shape[2], 3 * k.shape[3])
    flip = lambda k: k[::-1, ::-1].transpose(0, 3, 1, 2).reshape(3 * k.shape[3], 3 * k.shape[2])
    wide_rows = frames * (rows + 2) * cols
    narrow_rows = frames * rows * cols
    each = 2 * 9 * chans * state_chans
    weight_scale = 1.0 / math.sqrt(devices * narrow_rows * seqs)
    decay_scale = 1.0 / math.sqrt(seqs * rows * cols * sizes["rows"] * sizes["dp"])

    first, second = halo_pair(video, 2)
    wide, local, end = call(
        drive_kernel,
        [
            shape((frames, rows + 4, cols, chans), BF),
            shape((frames, rows + 2, cols, state_chans), F32),
            shape((rows + 2, cols, state_chans), BF),
        ],
        [edge, video, first, second, flat(in_kernel), lam],
        1,
        flops=each * wide_rows,
    )
    carry = from_earlier(end, totals)
    state, act, grad, gain_part = call(
        layer_kernel,
        [
            shape((frames, rows + 2, cols, state_chans), BF),
            shape(video.shape, BF),
            shape(video.shape, BF),
            shape((1, chans), F32),
        ],
        [local, carry, reach, video, cotangent, flat(out_kernel), gain],
        0,
        flops=each * narrow_rows,
    )
    first, second = halo_pair(grad, 2)
    (out_part,) = call(
        functools.partial(out_grad_kernel, weight_scale),
        [shape((3, 3, state_chans, chans), F32)],
        [state, grad],
        0,
        scratch=[pltpu.VMEM((3 * state_chans, 3 * chans), F32)],
        flops=each * narrow_rows,
    )
    local, lead = call(
        back_kernel,
        [
            shape((frames, rows + 2, cols, state_chans), F32),
            shape((rows + 2, cols, state_chans), BF),
        ],
        [edge, grad, first, second, flip(out_kernel), lam],
        1,
        scratch=[pltpu.VMEM((frames, rows + 4, cols, chans), BF)],
        flops=each * wide_rows,
    )
    back = from_later(lead, totals)
    adjoint, in_part, decay_part = call(
        functools.partial(in_grad_kernel, weight_scale, decay_scale),
        [
            shape((frames, rows + 2, cols, state_chans), BF),
            shape((3, 3, chans, state_chans), F32),
            shape((frames, 1, state_chans), F32),
        ],
        [local, back, back_reach, lam, wide, state, carry],
        0,
        scratch=[pltpu.VMEM((3 * chans, 3 * state_chans), F32)],
        flops=each * narrow_rows,
    )
    (video_grad,) = call(
        video_grad_kernel,
        [shape(video.shape, BF)],
        [adjoint, grad, flip(in_kernel), gain],
        0,
        flops=each * narrow_rows,
    )
    block = lax.axis_index("tm")
    slots = jnp.where(
        jnp.arange(sizes["tm"])[:, None, None] == block, decay_part[:, 0][None], 0.0
    ).reshape(-1, state_chans)
    pieces = [
        in_part.reshape(-1, state_chans),
        out_part.reshape(-1, chans),
        slots,
        gain_part * weight_scale,
    ]
    used = sum(p.shape[0] for p in pieces)
    pieces.append(jnp.zeros((-used % 64, chans), F32))
    total = tree_sum(jnp.concatenate(pieces, axis=0)).astype(F32)
    at = 0
    sums = []
    for piece in pieces[:4]:
        sums.append(lax.slice_in_dim(total, at, at + piece.shape[0], axis=0))
        at += piece.shape[0]
    return (
        act[None],
        video_grad[None],
        sums[0].reshape(3, 3, chans, state_chans),
        sums[1].reshape(3, 3, state_chans, chans),
        sums[3][0],
        lax.dynamic_slice_in_dim(sums[2], block * frames, frames, axis=0),
    )


def solution(mesh):
    placed = (
        P("dp", "tm", "rows", None, None),
        P("dp", "tm", "rows", None, None),
        P(),
        P(),
        P(),
        P("tm", None),
    )
    return jax.shard_map(
        on_device,
        mesh=mesh,
        in_specs=placed,
        out_specs=(
            P("dp", "tm", "rows", None, None),
            P("dp", "tm", "rows", None, None),
            P(),
            P(),
            P(),
            P("tm", None),
        ),
        check_vma=False,
    )
```

```python
import functools
import math

import jax
import jax.numpy as jnp
from jax import lax
from jax.experimental import pallas as pl
from jax.experimental.pallas import tpu as pltpu
from jax.sharding import PartitionSpec as P

BF = jnp.bfloat16
F32 = jnp.float32
VMEM_LIMIT = 24 * 1024 * 1024
LAYER_GROUP = 8
LAST_GROUP = 8
OUTER_GROUP = 16
GELU_A = math.sqrt(2.0 / math.pi)
GELU_B = 0.044715


PLACES = {"s": pltpu.SMEM, "v": pltpu.VMEM, "h": pltpu.HBM}


def call(body, outs, ins, places, scratch=(), flops=0):
    moved = sum(math.prod(a.shape) * a.dtype.itemsize for a in list(ins) + list(outs))
    specs = [pl.BlockSpec(memory_space=PLACES[p]) for p in places]
    ins = [
        pltpu.with_memory_space_constraint(a, pltpu.HBM) if p == "h" else a for a, p in zip(ins, places)
    ]
    outs = [pltpu.HBM(a.shape, a.dtype) if p == "h" else a for a, p in zip(outs, places[len(ins) :])]
    return pl.pallas_call(
        body,
        out_shape=outs,
        in_specs=specs[: len(ins)],
        out_specs=specs[len(ins) :],
        scratch_shapes=list(scratch),
        compiler_params=pltpu.CompilerParams(vmem_limit_bytes=VMEM_LIMIT),
        cost_estimate=pl.CostEstimate(flops=flops, bytes_accessed=moved, transcendentals=0),
    )(*ins)


def piece_copy(source, target, sems, n, group):
    span = pl.ds(n * group, group)
    return pltpu.make_async_copy(source.at[span], target.at[span], sems.at[n])


def held(array):
    return pltpu.VMEM(array.shape, array.dtype)


def shape(dims, dtype):
    return jax.ShapeDtypeStruct(tuple(dims), dtype)


def columns(count, width, lanes):
    return lax.rem(lax.broadcasted_iota(jnp.int32, (count, lanes), 0), width)


def from_left(field, column):
    return jnp.where(column == 0, 0.0, pltpu.roll(field, 1, 0))


def from_right(field, column, width):
    return jnp.where(column == width - 1, 0.0, pltpu.roll(field, field.shape[0] - 1, 0))


def taps(field, first, rows):
    frames, _, cols, chans = field.shape
    return jnp.concatenate(
        [field[:, first + i : first + i + rows].reshape(frames * rows * cols, chans) for i in range(3)],
        axis=1,
    )


def conv(field, first, rows, weights):
    _, _, cols, _ = field.shape
    out = weights.shape[1] // 3
    wide = jnp.dot(taps(field, first, rows), weights, preferred_element_type=F32)
    column = columns(wide.shape[0], cols, out)
    return (
        wide[:, out : 2 * out]
        + from_left(wide[:, :out], column)
        + from_right(wide[:, 2 * out :], column, cols)
    )


def spread(grad, cols):
    column = columns(grad.shape[0], cols, grad.shape[1])
    return jnp.concatenate(
        [
            from_right(grad, column, cols).astype(BF),
            grad.astype(BF),
            from_left(grad, column).astype(BF),
        ],
        axis=1,
    )


def outer(left, right):
    return lax.dot_general(left, right, (((0,), (0,)), ((), ())), preferred_element_type=F32)


def group_of(frames, most):
    size = most
    while frames % size:
        size -= 1
    return size


def fill_halo(edge_ref, wide_ref, own_ref, first_ref, second_ref):
    rows, deep = own_ref.shape[1], first_ref.shape[1]
    odd = edge_ref[2] == 1
    wide_ref[:, deep : deep + rows] = own_ref[...]
    wide_ref[:, pl.ds(jnp.where(odd, 0, rows + deep), deep)] = first_ref[...]
    wide_ref[:, pl.ds(jnp.where(odd, rows + deep, 0), deep)] = second_ref[...]


def inside(edge_ref, field, width):
    count = field.shape[0]
    upper = jnp.where(edge_ref[0] == 1, field[:width], 0.0)
    lower = jnp.where(edge_ref[1] == 1, field[count - width :], 0.0)
    return jnp.concatenate([upper, field[width : count - width], lower], axis=0)


def drive_kernel(
    edge_ref, own_ref, first_ref, second_ref, kernel_ref, lam_ref,
    kept_ref, local_ref, end_ref, wide_ref, sem,
):
    frames, rows, cols, _ = own_ref.shape
    state_chans = kernel_ref.shape[1] // 3
    fill_halo(edge_ref, wide_ref, own_ref, first_ref, second_ref)
    keep = pltpu.make_async_copy(wide_ref, kept_ref, sem)
    keep.start()
    group = group_of(frames, 16)
    many = (rows + 2) * cols

    def step(n, state):
        base = n * group
        drive = conv(wide_ref[pl.ds(base, group)], 0, rows + 2, kernel_ref[...])
        for k in range(group):
            now = inside(edge_ref, drive[k * many : (k + 1) * many], cols)
            state = lam_ref[base + k] * state + now
            local_ref[base + k] = state.reshape(rows + 2, cols, state_chans)
        return state

    last = lax.fori_loop(0, frames // group, step, jnp.zeros((many, state_chans), F32))
    end_ref[...] = last.reshape(rows + 2, cols, state_chans).astype(BF)
    keep.wait()


def layer_kernel(
    local_ref, carry_ref, reach_ref, own_ref, cot_ref, kernel_ref, gain_ref,
    state_out, act_out, grad_ref, gain_grad_ref,
    own_in, cot_in, state_ref, act_ref, sems,
):
    frames, rows, cols, chans = own_ref.shape
    group = group_of(frames, LAYER_GROUP)
    many = group * rows * cols
    carry = carry_ref[...].astype(F32)
    steps = frames // group

    def start(n, _):
        piece_copy(own_ref, own_in, sems.at[0], n, group).start()
        piece_copy(cot_ref, cot_in, sems.at[1], n, group).start()
        return 0

    lax.fori_loop(0, steps, start, 0)

    def step(n, total):
        base = n * group
        state = jnp.stack(
            [(local_ref[base + k] + reach_ref[base + k] * carry).astype(BF) for k in range(group)]
        )
        state_ref[pl.ds(base, group)] = state
        piece_copy(state_ref, state_out, sems.at[2], n, group).start()
        flow = conv(state, 0, rows, kernel_ref[...])
        piece_copy(own_ref, own_in, sems.at[0], n, group).wait()
        piece_copy(cot_ref, cot_in, sems.at[1], n, group).wait()
        own = own_in[pl.ds(base, group)].reshape(many, chans).astype(F32)
        pre = flow + gain_ref[...] * own
        square = pre * pre
        bend = jnp.tanh(GELU_A * (pre + GELU_B * square * pre))
        half = 0.5 * (1.0 + bend)
        slope = half + 0.5 * pre * (1.0 - bend * bend) * (GELU_A * (1.0 + 3.0 * GELU_B * square))
        grad = cot_in[pl.ds(base, group)].reshape(many, chans).astype(F32) * slope
        act_ref[pl.ds(base, group)] = (pre * half).astype(BF).reshape(group, rows, cols, chans)
        piece_copy(act_ref, act_out, sems.at[3], n, group).start()
        grad_ref[pl.ds(base, group)] = grad.astype(BF).reshape(group, rows, cols, chans)
        return total + jnp.sum((grad * own).reshape(many // 8, 8, chans), axis=0)

    total = lax.fori_loop(0, steps, step, jnp.zeros((8, chans), F32))
    gain_grad_ref[...] = jnp.sum(total, axis=0, keepdims=True)

    def finish(n, _):
        piece_copy(state_ref, state_out, sems.at[2], n, group).wait()
        piece_copy(act_ref, act_out, sems.at[3], n, group).wait()
        return 0

    lax.fori_loop(0, steps, finish, 0)


def put_blocks(total_ref, out_ref, scale):
    left, right = total_ref.shape[0] // 3, total_ref.shape[1] // 3
    for i in range(3):
        for j in range(3):
            at = (3 * i + j) * left
            out_ref[at : at + left] = (
                total_ref[i * left : (i + 1) * left, j * right : (j + 1) * right] * scale
            )


def out_grad_kernel(scale, state_ref, grad_ref, out_ref, total_ref):
    frames, rows, cols, chans = grad_ref.shape
    group = group_of(frames, 16)
    total_ref[...] = jnp.zeros_like(total_ref)

    def step(n, _):
        base = n * group
        grad = grad_ref[pl.ds(base, group)].reshape(group * rows * cols, chans).astype(F32)
        left = taps(state_ref[pl.ds(base, group)], 0, rows)
        total_ref[...] += outer(left, spread(grad, cols))
        return 0

    lax.fori_loop(0, frames // group, step, 0)
    put_blocks(total_ref, out_ref, scale)


def back_kernel(edge_ref, own_ref, first_ref, second_ref, kernel_ref, lam_ref, local_ref, lead_ref, wide_ref):
    frames, rows, cols, _ = own_ref.shape
    state_chans = kernel_ref.shape[1] // 3
    fill_halo(edge_ref, wide_ref, own_ref, first_ref, second_ref)
    group = group_of(frames, 16)
    many = (rows + 2) * cols

    def step(n, carry):
        base = frames - (n + 1) * group
        flow = conv(wide_ref[pl.ds(base, group)], 0, rows + 2, kernel_ref[...])
        for k in reversed(range(group)):
            adjoint = inside(edge_ref, flow[k * many : (k + 1) * many], cols) + carry
            local_ref[base + k] = adjoint.reshape(rows + 2, cols, state_chans)
            carry = lam_ref[base + k] * adjoint
        return carry

    lead = lax.fori_loop(0, frames // group, step, jnp.zeros((many, state_chans), F32))
    lead_ref[...] = lead.reshape(rows + 2, cols, state_chans).astype(BF)


def in_grad_kernel(
    scale, decay_scale, blocks, place_ref, local_ref, back_ref, reach_ref, lam_ref, wide_ref, state_ref,
    carry_ref, other_ref, gain_ref,
    adjoint_out, sent_ref, kept_ref, total_ref, adjoint_ref, mine_ref, decay_ref, sems,
):
    frames, rows_two, cols, chans = local_ref.shape
    rows = rows_two - 2
    group = group_of(frames, OUTER_GROUP)
    many = rows * cols
    back = back_ref[...].astype(F32)
    total_ref[...] = jnp.zeros_like(total_ref)

    def step(n, previous):
        base = n * group
        kept = []
        for k in range(group):
            adjoint = local_ref[base + k] + reach_ref[base + k] * back
            adjoint_ref[base + k] = adjoint.astype(BF)
            mine = adjoint[1 : 1 + rows].reshape(many, chans)
            kept.append(mine)
            part = jnp.sum((mine * previous).reshape(many // 8, 8, chans), axis=0)
            decay_ref[pl.ds(base + k, 1)] = (
                jnp.sum(part, axis=0, keepdims=True) * lam_ref[base + k] * decay_scale
            )
            previous = state_ref[base + k, 1 : 1 + rows].reshape(many, chans).astype(F32)
        piece_copy(adjoint_ref, adjoint_out, sems, n, group).start()
        left = taps(wide_ref[pl.ds(base, group)], 1, rows)
        total_ref[...] += outer(left, spread(jnp.concatenate(kept, axis=0), cols))
        return previous

    before = carry_ref[1 : 1 + rows].reshape(many, chans).astype(F32)
    lax.fori_loop(0, frames // group, step, before)
    count, full = other_ref.shape[0], mine_ref.shape[0]
    used = count + blocks * frames
    put_blocks(total_ref, mine_ref, scale)
    for n in range(blocks):
        mine_ref[count + n * frames : count + (n + 1) * frames] = jnp.where(
            place_ref[1] == n, decay_ref[...], 0.0
        )
    if full > used:
        mine_ref[used:] = jnp.zeros((full - used, chans), F32)
    row = lax.broadcasted_iota(jnp.int32, (full - count, chans), 0)
    rest = jnp.where(row == 0, gain_ref[...] * scale, 0.0)

    @pl.when(place_ref[0] == 0)
    def _():
        kept_ref[...] = mine_ref[...]
        sent_ref[:count] = other_ref[...].astype(BF)
        sent_ref[count:] = rest.astype(BF)

    @pl.when(place_ref[0] != 0)
    def _():
        sent_ref[...] = mine_ref[...].astype(BF)
        kept_ref[:count] = other_ref[...]
        kept_ref[count:] = rest

    def finish(n, _):
        piece_copy(adjoint_ref, adjoint_out, sems, n, group).wait()
        return 0

    lax.fori_loop(0, frames // group, finish, 0)


def result_kernel(blocks, place_ref, own_ref, other_ref, in_ref, out_ref, gain_ref, decay_ref):
    frames, chans = decay_ref.shape
    size = in_ref.shape[2]
    count = 9 * size

    def put(first, second):
        for i in range(3):
            for j in range(3):
                at = (3 * i + j) * size
                in_ref[i, j] = first[at : at + size].astype(F32)
                out_ref[i, j] = second[at : at + size].astype(F32)
        gain_ref[...] = second[count : count + 16].astype(F32)[:1]
        decay = jnp.zeros((frames, chans), F32)
        for n in range(blocks):
            slot = first[count + n * frames : count + (n + 1) * frames].astype(F32)
            decay = jnp.where(place_ref[1] == n, slot, decay)
        decay_ref[...] = decay

    @pl.when(place_ref[0] == 0)
    def _():
        put(own_ref, other_ref)

    @pl.when(place_ref[0] != 0)
    def _():
        put(other_ref, own_ref)


def video_grad_kernel(adjoint_ref, grad_ref, kernel_ref, gain_ref, video_out, out_ref, sems):
    frames, rows, cols, chans = grad_ref.shape
    group = group_of(frames, LAST_GROUP)

    def step(n, _):
        base = n * group
        grad = grad_ref[pl.ds(base, group)].reshape(group * rows * cols, chans).astype(F32)
        flow = conv(adjoint_ref[pl.ds(base, group)], 0, rows, kernel_ref[...])
        out_ref[pl.ds(base, group)] = (
            (flow + gain_ref[...] * grad).astype(BF).reshape(group, rows, cols, chans)
        )
        piece_copy(out_ref, video_out, sems, n, group).start()
        return 0

    def finish(n, _):
        piece_copy(out_ref, video_out, sems, n, group).wait()
        return 0

    lax.fori_loop(0, frames // group, step, 0)
    lax.fori_loop(0, frames // group, finish, 0)


def halo_pair(field, deep):
    count = lax.axis_size("rows")
    odd = lax.rem(lax.axis_index("rows"), 2)
    rows = field.shape[1]
    swap = lambda low: [p for i in range(low, count - 1, 2) for p in ((i, i + 1), (i + 1, i))]
    pick = lambda flag: lax.dynamic_slice_in_dim(field, flag * (rows - deep), deep, axis=1)
    first, second = pick(1 - odd), pick(odd)
    return lax.ppermute(first, "rows", swap(0)), lax.ppermute(second, "rows", swap(1))


def from_earlier(end, totals):
    count = lax.axis_size("tm")
    found, between = None, None
    for k in range(1, count):
        pairs = [(i, i + k) for i in range(count - k)]
        piece = lax.ppermute(end, "tm", pairs)
        if k == 1:
            found = piece.astype(F32)
        else:
            step = lax.ppermute(totals, "tm", [(i, i + k - 1) for i in range(count - k + 1)])
            between = step if between is None else between + step
            found = found + jnp.exp(between) * piece.astype(F32)
    if found is None:
        return jnp.zeros(end.shape, BF)
    return found.astype(BF)


def from_later(lead, totals):
    count = lax.axis_size("tm")
    found, between = None, None
    for k in range(1, count):
        pairs = [(i + k, i) for i in range(count - k)]
        piece = lax.ppermute(lead, "tm", pairs)
        if k == 1:
            found = piece.astype(F32)
        else:
            step = lax.ppermute(totals, "tm", [(i + k - 1, i) for i in range(count - k + 1)])
            between = step if between is None else between + step
            found = found + jnp.exp(between) * piece.astype(F32)
    if found is None:
        return jnp.zeros(lead.shape, BF)
    return found.astype(BF)


def tree_sum(sent, kept):
    axes = ("tm", "rows", "dp")
    bits, devices = [], 1
    for axis in reversed(axes):
        size = 1
        while size < lax.axis_size(axis):
            bits.append((axis, size, size * devices))
            size *= 2
        devices *= lax.axis_size(axis)
    halves = [b for b in bits if b[0] == "dp"][0]
    group = [b for b in bits if b[0] == "dp"][1:2] + [b for b in bits if b[0] == "tm"][:1]
    far = [b for b in bits if b != halves and b not in group]

    def swap(value, mask):
        return lax.ppermute(value, axes, [(i, i ^ mask) for i in range(devices)])

    def combined(k):
        return sum(mask for n, (_, _, mask) in enumerate(group) if (k >> n) & 1)

    spot = 0
    for n, (axis, mask, _) in enumerate(group):
        spot = spot + jnp.where((lax.axis_index(axis) & mask) != 0, 1 << n, 0)
    ways = 1 << len(group)
    size = kept.shape[0] // ways
    half = kept + swap(sent, halves[2]).astype(F32)
    chunk = lambda k: lax.dynamic_slice_in_dim(half, (spot ^ k) * size, size, axis=0)
    chunks = lax.optimization_barrier([chunk(0)] + [chunk(k).astype(BF) for k in range(1, ways)])
    found = [swap(chunks[k], combined(k)) for k in range(1, ways)]
    total = chunks[0]
    for piece in found:
        total = total + piece.astype(F32)
    total = total.astype(BF)
    for _, _, mask in far:
        total = (total.astype(F32) + swap(total, mask).astype(F32)).astype(BF)
    found = [total] + [swap(total, combined(k)) for k in range(1, ways)]
    own = jnp.zeros(sent.shape, BF)
    for k, piece in enumerate(found):
        own = lax.dynamic_update_slice_in_dim(own, piece, (spot ^ k) * size, axis=0)
    return own, swap(own, halves[2])


def on_device(video, cotangent, in_kernel, out_kernel, skip_gain, log_decay):
    seqs, frames, rows, cols, chans = video.shape
    state_chans = in_kernel.shape[3]
    sizes = {axis: lax.axis_size(axis) for axis in ("tm", "rows", "dp")}
    devices = sizes["tm"] * sizes["rows"] * sizes["dp"]
    for size in sizes.values():
        assert size & (size - 1) == 0
    assert seqs == 1 and rows >= 2 and sizes["dp"] >= 2 and chans == state_chans
    video, cotangent = video[0], cotangent[0]
    band = lax.axis_index("rows")
    edge = jnp.stack(
        [jnp.where(band > 0, 1, 0), jnp.where(band < sizes["rows"] - 1, 1, 0), lax.rem(band, 2)]
    ).astype(jnp.int32)
    cum = jnp.cumsum(log_decay, axis=0)
    totals = cum[-1:]
    lam = jnp.exp(log_decay)[:, None, :]
    reach = jnp.exp(cum)[:, None, :]
    back_reach = jnp.exp(totals - cum)[:, None, :]
    gain = skip_gain[None, :]
    flat = lambda k: k.transpose(0, 2, 1, 3).reshape(3 * k.shape[2], 3 * k.shape[3])
    flip = lambda k: k[::-1, ::-1].transpose(0, 3, 1, 2).reshape(3 * k.shape[3], 3 * k.shape[2])
    wide_rows = frames * (rows + 2) * cols
    narrow_rows = frames * rows * cols
    each = 2 * 9 * chans * state_chans
    weight_scale = 1.0 / math.sqrt(devices * narrow_rows * seqs)
    decay_scale = 1.0 / math.sqrt(seqs * rows * cols * sizes["rows"] * sizes["dp"])

    first, second = halo_pair(video, 2)
    wide, local, end = call(
        drive_kernel,
        [
            shape((frames, rows + 4, cols, chans), BF),
            shape((frames, rows + 2, cols, state_chans), F32),
            shape((rows + 2, cols, state_chans), BF),
        ],
        [edge, video, first, second, flat(in_kernel), lam],
        "svvvvv" + "hvv",
        scratch=[
            pltpu.VMEM((frames, rows + 4, cols, chans), BF),
            pltpu.SemaphoreType.DMA(()),
        ],
        flops=each * wide_rows,
    )
    carry = from_earlier(end, totals)
    state, act, grad, gain_part = call(
        layer_kernel,
        [
            shape((frames, rows + 2, cols, state_chans), BF),
            shape(video.shape, BF),
            shape(video.shape, BF),
            shape((1, chans), F32),
        ],
        [local, carry, reach, video, cotangent, flat(out_kernel), gain],
        "vvvhhvv" + "hhvv",
        scratch=[
            held(video),
            held(video),
            pltpu.VMEM((frames, rows + 2, cols, state_chans), BF),
            held(video),
            pltpu.SemaphoreType.DMA((4, frames // group_of(frames, LAYER_GROUP))),
        ],
        flops=each * narrow_rows,
    )
    first, second = halo_pair(grad, 2)
    (out_part,) = call(
        functools.partial(out_grad_kernel, weight_scale),
        [shape((9 * state_chans, chans), F32)],
        [state, grad],
        "vvv",
        scratch=[pltpu.VMEM((3 * state_chans, 3 * chans), F32)],
        flops=each * narrow_rows,
    )
    local, lead = call(
        back_kernel,
        [
            shape((frames, rows + 2, cols, state_chans), F32),
            shape((rows + 2, cols, state_chans), BF),
        ],
        [edge, grad, first, second, flip(out_kernel), lam],
        "svvvvv" + "vv",
        scratch=[pltpu.VMEM((frames, rows + 4, cols, chans), BF)],
        flops=each * wide_rows,
    )
    back = from_later(lead, totals)
    blocks = sizes["tm"]
    full = 9 * chans + blocks * frames
    full += -full % 64 if full % 32 else 0
    place = jnp.stack([lax.rem(lax.axis_index("dp"), 2), lax.axis_index("tm")]).astype(jnp.int32)
    adjoint, sent, kept = call(
        functools.partial(in_grad_kernel, weight_scale, decay_scale, blocks),
        [
            shape((frames, rows + 2, cols, state_chans), BF),
            shape((full, chans), BF),
            shape((full, chans), F32),
        ],
        [place, local, back, back_reach, lam, wide, state, carry, out_part, gain_part],
        "svvvvvvvvv" + "hvv",
        scratch=[
            pltpu.VMEM((3 * chans, 3 * state_chans), F32),
            pltpu.VMEM((frames, rows + 2, cols, state_chans), BF),
            pltpu.VMEM((full, chans), F32),
            pltpu.VMEM((frames, state_chans), F32),
            pltpu.SemaphoreType.DMA((frames // group_of(frames, OUTER_GROUP),)),
        ],
        flops=each * narrow_rows,
    )
    (video_grad,) = call(
        video_grad_kernel,
        [shape(video.shape, BF)],
        [adjoint, grad, flip(in_kernel), gain],
        "vvvv" + "h",
        scratch=[
            held(video),
            pltpu.SemaphoreType.DMA((frames // group_of(frames, LAST_GROUP),)),
        ],
        flops=each * narrow_rows,
    )
    own, other = tree_sum(sent, kept)
    in_grad, out_grad, gain_grad, decay_grad = call(
        functools.partial(result_kernel, blocks),
        [
            shape((3, 3, chans, state_chans), F32),
            shape((3, 3, state_chans, chans), F32),
            shape((1, chans), F32),
            shape((frames, state_chans), F32),
        ],
        [place, own, other],
        "svv" + "vvvv",
    )
    return act[None], video_grad[None], in_grad, out_grad, gain_grad[0], decay_grad


def solution(mesh):
    placed = (
        P("dp", "tm", "rows", None, None),
        P("dp", "tm", "rows", None, None),
        P(),
        P(),
        P(),
        P("tm", None),
    )
    return jax.shard_map(
        on_device,
        mesh=mesh,
        in_specs=placed,
        out_specs=(
            P("dp", "tm", "rows", None, None),
            P("dp", "tm", "rows", None, None),
            P(),
            P(),
            P(),
            P("tm", None),
        ),
        check_vma=False,
    )
```

```python
import functools
import math

import jax
import jax.numpy as jnp
from jax import lax
from jax.experimental import pallas as pl
from jax.experimental.pallas import tpu as pltpu
from jax.sharding import PartitionSpec as P

BF = jnp.bfloat16
F32 = jnp.float32
VMEM_LIMIT = 24 * 1024 * 1024
LAYER_GROUP = 8
LAST_GROUP = 8
OUTER_GROUP = 16
NEAR_GROUP = 8
SCAN_GROUP = 4
GELU_A = math.sqrt(2.0 / math.pi)
GELU_B = 0.044715


PLACES = {"s": pltpu.SMEM, "v": pltpu.VMEM, "h": pltpu.HBM}


def call(body, outs, ins, places, scratch=(), flops=0, aliases=()):
    moved = sum(math.prod(a.shape) * a.dtype.itemsize for a in list(ins) + list(outs))
    specs = [pl.BlockSpec(memory_space=PLACES[p]) for p in places]
    ins = [
        pltpu.with_memory_space_constraint(a, pltpu.HBM) if p == "h" else a for a, p in zip(ins, places)
    ]
    outs = [pltpu.HBM(a.shape, a.dtype) if p == "h" else a for a, p in zip(outs, places[len(ins) :])]
    return pl.pallas_call(
        body,
        out_shape=outs,
        in_specs=specs[: len(ins)],
        out_specs=specs[len(ins) :],
        scratch_shapes=list(scratch),
        input_output_aliases=dict(aliases),
        compiler_params=pltpu.CompilerParams(vmem_limit_bytes=VMEM_LIMIT),
        cost_estimate=pl.CostEstimate(flops=flops, bytes_accessed=moved, transcendentals=0),
    )(*ins)


def piece_copy(source, target, sems, n, group):
    span = pl.ds(n * group, group)
    return pltpu.make_async_copy(source.at[span], target.at[span], sems.at[n])


def held(array):
    return pltpu.VMEM(array.shape, array.dtype)


def shape(dims, dtype):
    return jax.ShapeDtypeStruct(tuple(dims), dtype)


def columns(count, width, lanes):
    return lax.rem(lax.broadcasted_iota(jnp.int32, (count, lanes), 0), width)


def from_left(field, column):
    return jnp.where(column == 0, 0.0, pltpu.roll(field, 1, 0))


def from_right(field, column, width):
    return jnp.where(column == width - 1, 0.0, pltpu.roll(field, field.shape[0] - 1, 0))


def taps(field, first, rows):
    frames, _, cols, chans = field.shape
    return jnp.concatenate(
        [field[:, first + i : first + i + rows].reshape(frames * rows * cols, chans) for i in range(3)],
        axis=1,
    )


def conv(field, first, rows, weights):
    _, _, cols, _ = field.shape
    out = weights.shape[1] // 3
    wide = jnp.dot(taps(field, first, rows), weights, preferred_element_type=F32)
    column = columns(wide.shape[0], cols, out)
    return (
        wide[:, out : 2 * out]
        + from_left(wide[:, :out], column)
        + from_right(wide[:, 2 * out :], column, cols)
    )


def spread(grad, cols):
    column = columns(grad.shape[0], cols, grad.shape[1])
    return jnp.concatenate(
        [
            from_right(grad, column, cols).astype(BF),
            grad.astype(BF),
            from_left(grad, column).astype(BF),
        ],
        axis=1,
    )


def outer(left, right):
    return lax.dot_general(left, right, (((0,), (0,)), ((), ())), preferred_element_type=F32)


def group_of(frames, most):
    size = most
    while frames % size:
        size -= 1
    return size


def fill_halo(wide_ref, own_ref, first_ref, second_ref):
    rows, deep = own_ref.shape[1], first_ref.shape[1]
    odd = lax.rem(lax.axis_index("rows"), 2) == 1
    wide_ref[:, deep : deep + rows] = own_ref[...]
    wide_ref[:, pl.ds(jnp.where(odd, 0, rows + deep), deep)] = first_ref[...]
    wide_ref[:, pl.ds(jnp.where(odd, rows + deep, 0), deep)] = second_ref[...]


def inside(field, width):
    count = field.shape[0]
    upper = jnp.where(lax.axis_index("rows") > 0, field[:width], 0.0)
    lower = jnp.where(lax.axis_index("rows") < lax.axis_size("rows") - 1, field[count - width :], 0.0)
    return jnp.concatenate([upper, field[width : count - width], lower], axis=0)


def near_kernel(own_ref, kernel_ref, near_ref, wide_ref):
    frames, rows, cols, chans = own_ref.shape
    group = group_of(frames, NEAR_GROUP)
    none = jnp.zeros((group, 2, cols, chans), BF)

    def step(n, _):
        span = pl.ds(n * group, group)
        wide_ref[:, :2] = none
        wide_ref[:, 2 : 2 + rows] = own_ref[span]
        wide_ref[:, 2 + rows :] = none
        near = conv(wide_ref[...], 0, rows + 2, kernel_ref[...])
        near_ref[span] = near.reshape(group, rows + 2, cols, near.shape[1])
        return 0

    lax.fori_loop(0, frames // group, step, 0)


def halo_part(first_ref, second_ref, kernel_ref, upper_ref, lower_ref):
    frames, deep, cols, chans = first_ref.shape
    state_chans = kernel_ref.shape[1] // 3
    odd = lax.rem(lax.axis_index("rows"), 2) == 1

    def put(out_ref, left, right, weights):
        pair = jnp.concatenate([left, right], axis=3).reshape(frames * deep * cols, 2 * chans)
        wide = jnp.dot(pair, weights, preferred_element_type=F32)
        column = columns(wide.shape[0], cols, state_chans)
        out_ref[...] = (
            wide[:, state_chans : 2 * state_chans]
            + from_left(wide[:, :state_chans], column)
            + from_right(wide[:, 2 * state_chans :], column, cols)
        ).reshape(frames, deep, cols, state_chans)

    def both(above_ref, below_ref):
        none = jnp.zeros((frames, 1, cols, chans), BF)
        above, below = above_ref[...], below_ref[...]
        put(upper_ref, above, jnp.concatenate([above[:, 1:], none], axis=1), kernel_ref[: 2 * chans])
        put(lower_ref, jnp.concatenate([none, below[:, :1]], axis=1), below, kernel_ref[chans:])

    @pl.when(odd)
    def _():
        both(first_ref, second_ref)

    @pl.when(jnp.logical_not(odd))
    def _():
        both(second_ref, first_ref)


def whole_rows(near, upper, lower):
    count, cols, chans = near.shape
    field = jnp.concatenate([near[:2] + upper, near[2 : count - 2], near[count - 2 :] + lower], axis=0)
    return inside(field.reshape(count * cols, chans), cols)


def drive_kernel(
    near_ref, own_ref, first_ref, second_ref, kernel_ref, lam_ref,
    kept_ref, local_ref, end_ref, wide_ref, upper_ref, lower_ref, sem,
):
    frames, rows_two, cols, state_chans = near_ref.shape
    fill_halo(wide_ref, own_ref, first_ref, second_ref)
    keep = pltpu.make_async_copy(wide_ref, kept_ref, sem)
    keep.start()
    halo_part(first_ref, second_ref, kernel_ref, upper_ref, lower_ref)
    group = group_of(frames, SCAN_GROUP)

    def step(n, state):
        for k in range(group):
            t = n * group + k
            state = lam_ref[t] * state + whole_rows(near_ref[t], upper_ref[t], lower_ref[t])
            local_ref[t] = state.reshape(rows_two, cols, state_chans)
        return state

    last = lax.fori_loop(0, frames // group, step, jnp.zeros((rows_two * cols, state_chans), F32))
    end_ref[...] = last.reshape(rows_two, cols, state_chans).astype(BF)
    keep.wait()


def layer_kernel(
    local_ref, carry_ref, reach_ref, own_ref, cot_ref, kernel_ref, gain_ref,
    state_out, act_out, grad_ref, gain_grad_ref,
    own_in, cot_in, state_ref, act_ref, sems,
):
    frames, rows, cols, chans = own_ref.shape
    group = group_of(frames, LAYER_GROUP)
    many = group * rows * cols
    carry = carry_ref[...].astype(F32)
    steps = frames // group

    def start(n, _):
        piece_copy(own_ref, own_in, sems.at[0], n, group).start()
        piece_copy(cot_ref, cot_in, sems.at[1], n, group).start()
        return 0

    lax.fori_loop(0, steps, start, 0)

    def step(n, total):
        base = n * group
        state = jnp.stack(
            [(local_ref[base + k] + reach_ref[base + k] * carry).astype(BF) for k in range(group)]
        )
        state_ref[pl.ds(base, group)] = state
        piece_copy(state_ref, state_out, sems.at[2], n, group).start()
        flow = conv(state, 0, rows, kernel_ref[...])
        piece_copy(own_ref, own_in, sems.at[0], n, group).wait()
        piece_copy(cot_ref, cot_in, sems.at[1], n, group).wait()
        own = own_in[pl.ds(base, group)].reshape(many, chans).astype(F32)
        pre = flow + gain_ref[...] * own
        square = pre * pre
        bend = jnp.tanh(GELU_A * (pre + GELU_B * square * pre))
        half = 0.5 * (1.0 + bend)
        slope = half + 0.5 * pre * (1.0 - bend * bend) * (GELU_A * (1.0 + 3.0 * GELU_B * square))
        grad = cot_in[pl.ds(base, group)].reshape(many, chans).astype(F32) * slope
        act_ref[pl.ds(base, group)] = (pre * half).astype(BF).reshape(group, rows, cols, chans)
        piece_copy(act_ref, act_out, sems.at[3], n, group).start()
        grad_ref[pl.ds(base, group)] = grad.astype(BF).reshape(group, rows, cols, chans)
        return total + jnp.sum((grad * own).reshape(many // 8, 8, chans), axis=0)

    total = lax.fori_loop(0, steps, step, jnp.zeros((8, chans), F32))
    gain_grad_ref[...] = jnp.sum(total, axis=0, keepdims=True)

    def finish(n, _):
        piece_copy(state_ref, state_out, sems.at[2], n, group).wait()
        piece_copy(act_ref, act_out, sems.at[3], n, group).wait()
        return 0

    lax.fori_loop(0, steps, finish, 0)


def put_blocks(total_ref, out_ref, scale):
    left, right = total_ref.shape[0] // 3, total_ref.shape[1] // 3
    for i in range(3):
        for j in range(3):
            at = (3 * i + j) * left
            out_ref[at : at + left] = (
                total_ref[i * left : (i + 1) * left, j * right : (j + 1) * right] * scale
            )


def out_grad_kernel(scale, state_ref, grad_ref, out_ref, total_ref):
    frames, rows, cols, chans = grad_ref.shape
    group = group_of(frames, 16)
    total_ref[...] = jnp.zeros_like(total_ref)

    def step(n, _):
        base = n * group
        grad = grad_ref[pl.ds(base, group)].reshape(group * rows * cols, chans).astype(F32)
        left = taps(state_ref[pl.ds(base, group)], 0, rows)
        total_ref[...] += outer(left, spread(grad, cols))
        return 0

    lax.fori_loop(0, frames // group, step, 0)
    put_blocks(total_ref, out_ref, scale)


def back_kernel(
    near_ref, first_ref, second_ref, kernel_ref, lam_ref,
    local_ref, lead_ref, upper_ref, lower_ref,
):
    frames, rows_two, cols, state_chans = near_ref.shape
    halo_part(first_ref, second_ref, kernel_ref, upper_ref, lower_ref)
    group = group_of(frames, SCAN_GROUP)

    def step(n, carry):
        for k in range(group):
            t = frames - 1 - (n * group + k)
            adjoint = whole_rows(near_ref[t], upper_ref[t], lower_ref[t]) + carry
            local_ref[t] = adjoint.reshape(rows_two, cols, state_chans)
            carry = lam_ref[t] * adjoint
        return carry

    lead = lax.fori_loop(0, frames // group, step, jnp.zeros((rows_two * cols, state_chans), F32))
    lead_ref[...] = lead.reshape(rows_two, cols, state_chans).astype(BF)


def in_grad_kernel(
    scale, decay_scale, blocks, local_ref, back_ref, reach_ref, lam_ref, wide_ref, state_ref,
    carry_ref, other_ref, gain_ref,
    adjoint_ref, sent_ref, kept_ref, total_ref, mine_ref, decay_ref,
):
    frames, rows_two, cols, chans = local_ref.shape
    rows = rows_two - 2
    group = group_of(frames, OUTER_GROUP)
    many = rows * cols
    back = back_ref[...].astype(F32)
    alone = group == frames

    def step(n, previous):
        base = n * group
        kept = []
        for k in range(group):
            adjoint = local_ref[base + k] + reach_ref[base + k] * back
            adjoint_ref[base + k] = adjoint.astype(BF)
            mine = adjoint[1 : 1 + rows].reshape(many, chans)
            kept.append(mine)
            part = jnp.sum((mine * previous).reshape(many // 8, 8, chans), axis=0)
            decay_ref[pl.ds(base + k, 1)] = (
                jnp.sum(part, axis=0, keepdims=True) * lam_ref[base + k] * decay_scale
            )
            previous = state_ref[base + k, 1 : 1 + rows].reshape(many, chans).astype(F32)
        left = taps(wide_ref[pl.ds(base, group)], 1, rows)
        found = outer(left, spread(jnp.concatenate(kept, axis=0), cols))
        total_ref[...] = found if alone else jnp.where(n == 0, found, total_ref[...] + found)
        return previous

    before = carry_ref[1 : 1 + rows].reshape(many, chans).astype(F32)
    if alone:
        step(0, before)
    else:
        lax.fori_loop(0, frames // group, step, before)
    count, full = other_ref.shape[0], mine_ref.shape[0]
    used = count + blocks * frames
    put_blocks(total_ref, mine_ref, scale)
    for n in range(blocks):
        mine_ref[count + n * frames : count + (n + 1) * frames] = jnp.where(
            lax.axis_index("tm") == n, decay_ref[...], 0.0
        )
    if full > used:
        mine_ref[used:] = jnp.zeros((full - used, chans), F32)
    row = lax.broadcasted_iota(jnp.int32, (full - count, chans), 0)
    rest = jnp.where(row == 0, gain_ref[...] * scale, 0.0)

    @pl.when(lax.rem(lax.axis_index("dp"), 2) == 0)
    def _():
        kept_ref[...] = mine_ref[...]
        sent_ref[:count] = other_ref[...].astype(BF)
        sent_ref[count:] = rest.astype(BF)

    @pl.when(lax.rem(lax.axis_index("dp"), 2) != 0)
    def _():
        sent_ref[...] = mine_ref[...].astype(BF)
        kept_ref[:count] = other_ref[...]
        kept_ref[count:] = rest


def result_kernel(blocks, own_ref, other_ref, in_ref, out_ref, gain_ref, decay_ref):
    frames, chans = decay_ref.shape
    size = in_ref.shape[2]
    count = 9 * size

    def put(first, second):
        for i in range(3):
            for j in range(3):
                at = (3 * i + j) * size
                in_ref[i, j] = first[at : at + size].astype(F32)
                out_ref[i, j] = second[at : at + size].astype(F32)
        gain_ref[...] = second[count : count + 16].astype(F32)[:1]
        decay = jnp.zeros((frames, chans), F32)
        for n in range(blocks):
            slot = first[count + n * frames : count + (n + 1) * frames].astype(F32)
            decay = jnp.where(lax.axis_index("tm") == n, slot, decay)
        decay_ref[...] = decay

    @pl.when(lax.rem(lax.axis_index("dp"), 2) == 0)
    def _():
        put(own_ref, other_ref)

    @pl.when(lax.rem(lax.axis_index("dp"), 2) != 0)
    def _():
        put(other_ref, own_ref)


def video_grad_kernel(adjoint_ref, grad_ref, kernel_ref, gain_ref, video_out, out_ref, sems):
    frames, rows, cols, chans = grad_ref.shape
    group = group_of(frames, LAST_GROUP)

    def step(n, _):
        base = n * group
        grad = grad_ref[pl.ds(base, group)].reshape(group * rows * cols, chans).astype(F32)
        flow = conv(adjoint_ref[pl.ds(base, group)], 0, rows, kernel_ref[...])
        out_ref[pl.ds(base, group)] = (
            (flow + gain_ref[...] * grad).astype(BF).reshape(group, rows, cols, chans)
        )
        piece_copy(out_ref, video_out, sems, n, group).start()
        return 0

    def finish(n, _):
        piece_copy(out_ref, video_out, sems, n, group).wait()
        return 0

    lax.fori_loop(0, frames // group, step, 0)
    lax.fori_loop(0, frames // group, finish, 0)


def edge_kernel(field_ref, first_ref, second_ref, sems):
    deep = first_ref.shape[1]
    last = field_ref.shape[1] - deep
    odd = lax.rem(lax.axis_index("rows"), 2)
    one = pltpu.make_async_copy(field_ref.at[:, pl.ds((1 - odd) * last, deep)], first_ref, sems.at[0])
    two = pltpu.make_async_copy(field_ref.at[:, pl.ds(odd * last, deep)], second_ref, sems.at[1])
    one.start()
    two.start()
    one.wait()
    two.wait()


def halo_pair(field, deep, read=False):
    count = lax.axis_size("rows")
    odd = lax.rem(lax.axis_index("rows"), 2)
    rows = field.shape[1]
    swap = lambda low: [p for i in range(low, count - 1, 2) for p in ((i, i + 1), (i + 1, i))]
    pick = lambda flag: lax.dynamic_slice_in_dim(field, flag * (rows - deep), deep, axis=1)
    if read:
        edges = shape((field.shape[0], deep) + field.shape[2:], field.dtype)
        first, second = call(
            edge_kernel, [edges, edges], [field], "hvv", scratch=[pltpu.SemaphoreType.DMA((2,))]
        )
    else:
        first, second = pick(1 - odd), pick(odd)
    first = lax.ppermute(first, "rows", swap(0))
    second = lax.ppermute(second, "rows", swap(1))
    return first, second


def from_earlier(end, totals):
    count = lax.axis_size("tm")
    found, between = None, None
    for k in range(1, count):
        pairs = [(i, i + k) for i in range(count - k)]
        piece = lax.ppermute(end, "tm", pairs)
        if k == 1:
            found = piece.astype(F32)
        else:
            step = lax.ppermute(totals, "tm", [(i, i + k - 1) for i in range(count - k + 1)])
            between = step if between is None else between + step
            found = found + jnp.exp(between) * piece.astype(F32)
    if found is None:
        return jnp.zeros(end.shape, BF)
    return found.astype(BF)


def from_later(lead, totals):
    count = lax.axis_size("tm")
    found, between = None, None
    for k in range(1, count):
        pairs = [(i + k, i) for i in range(count - k)]
        piece = lax.ppermute(lead, "tm", pairs)
        if k == 1:
            found = piece.astype(F32)
        else:
            step = lax.ppermute(totals, "tm", [(i + k - 1, i) for i in range(count - k + 1)])
            between = step if between is None else between + step
            found = found + jnp.exp(between) * piece.astype(F32)
    if found is None:
        return jnp.zeros(lead.shape, BF)
    return found.astype(BF)


def tree_sum(sent, kept):
    axes = ("tm", "rows", "dp")
    bits, devices = [], 1
    for axis in reversed(axes):
        size = 1
        while size < lax.axis_size(axis):
            bits.append((axis, size, size * devices))
            size *= 2
        devices *= lax.axis_size(axis)
    halves = [b for b in bits if b[0] == "dp"][0]
    group = [b for b in bits if b[0] == "dp"][1:2] + [b for b in bits if b[0] == "tm"][:1]
    far = [b for b in bits if b != halves and b not in group]

    def swap(value, mask):
        return lax.ppermute(value, axes, [(i, i ^ mask) for i in range(devices)])

    def combined(k):
        return sum(mask for n, (_, _, mask) in enumerate(group) if (k >> n) & 1)

    spot = 0
    for n, (axis, mask, _) in enumerate(group):
        spot = spot + jnp.where((lax.axis_index(axis) & mask) != 0, 1 << n, 0)
    ways = 1 << len(group)
    size = kept.shape[0] // ways
    half = kept + swap(sent, halves[2]).astype(F32)
    chunk = lambda k: lax.dynamic_slice_in_dim(half, (spot ^ k) * size, size, axis=0)
    chunks = lax.optimization_barrier([chunk(0)] + [chunk(k).astype(BF) for k in range(1, ways)])
    found = [swap(chunks[k], combined(k)) for k in range(1, ways)]
    total = chunks[0]
    for piece in found:
        total = total + piece.astype(F32)
    total = total.astype(BF)
    for _, _, mask in far:
        total = (total.astype(F32) + swap(total, mask).astype(F32)).astype(BF)
    found = [total] + [swap(total, combined(k)) for k in range(1, ways)]
    own = jnp.zeros(sent.shape, BF)
    for k, piece in enumerate(found):
        own = lax.dynamic_update_slice_in_dim(own, piece, (spot ^ k) * size, axis=0)
    return own, swap(own, halves[2])


def on_device(video, cotangent, in_kernel, out_kernel, skip_gain, log_decay):
    seqs, frames, rows, cols, chans = video.shape
    state_chans = in_kernel.shape[3]
    sizes = {axis: lax.axis_size(axis) for axis in ("tm", "rows", "dp")}
    devices = sizes["tm"] * sizes["rows"] * sizes["dp"]
    for size in sizes.values():
        assert size & (size - 1) == 0
    assert seqs == 1 and rows >= 2 and sizes["dp"] >= 2 and chans == state_chans
    video, cotangent = video[0], cotangent[0]
    cum = jnp.cumsum(log_decay, axis=0)
    totals = cum[-1:]
    lam = jnp.exp(log_decay)[:, None, :]
    reach = jnp.exp(cum)[:, None, :]
    back_reach = jnp.exp(totals - cum)[:, None, :]
    gain = skip_gain[None, :]
    flat = lambda k: k.transpose(0, 2, 1, 3).reshape(3 * k.shape[2], 3 * k.shape[3])
    flip = lambda k: k[::-1, ::-1].transpose(0, 3, 1, 2).reshape(3 * k.shape[3], 3 * k.shape[2])
    wide_rows = frames * (rows + 2) * cols
    narrow_rows = frames * rows * cols
    each = 2 * 9 * chans * state_chans
    weight_scale = 1.0 / math.sqrt(devices * narrow_rows * seqs)
    decay_scale = 1.0 / math.sqrt(seqs * rows * cols * sizes["rows"] * sizes["dp"])

    first, second = halo_pair(video, 2, True)
    near_shape = shape((frames, rows + 2, cols, state_chans), F32)
    near_scratch = [pltpu.VMEM((group_of(frames, NEAR_GROUP), rows + 4, cols, chans), BF)]
    halo_scratch = [pltpu.VMEM((frames, 2, cols, state_chans), F32)] * 2
    (near,) = call(
        near_kernel, [near_shape], [video, flat(in_kernel)], "vvv",
        scratch=near_scratch, flops=each * wide_rows,
    )
    wide, local, end = call(
        drive_kernel,
        [
            shape((frames, rows + 4, cols, chans), BF),
            near_shape,
            shape((rows + 2, cols, state_chans), BF),
        ],
        [near, video, first, second, flat(in_kernel), lam],
        "vvvvvv" + "hvv",
        scratch=[
            pltpu.VMEM((frames, rows + 4, cols, chans), BF),
            *halo_scratch,
            pltpu.SemaphoreType.DMA(()),
        ],
        flops=each * narrow_rows // 3,
        aliases=((0, 1),),
    )
    carry = from_earlier(end, totals)
    state, act, grad, gain_part = call(
        layer_kernel,
        [
            shape((frames, rows + 2, cols, state_chans), BF),
            shape(video.shape, BF),
            shape(video.shape, BF),
            shape((1, chans), F32),
        ],
        [local, carry, reach, video, cotangent, flat(out_kernel), gain],
        "vvvhhvv" + "hhvv",
        scratch=[
            held(video),
            held(video),
            pltpu.VMEM((frames, rows + 2, cols, state_chans), BF),
            held(video),
            pltpu.SemaphoreType.DMA((4, frames // group_of(frames, LAYER_GROUP))),
        ],
        flops=each * narrow_rows,
    )
    first, second = halo_pair(grad, 2)
    (near,) = call(
        near_kernel, [near_shape], [grad, flip(out_kernel)], "vvv",
        scratch=near_scratch, flops=each * wide_rows,
    )
    (out_part,) = call(
        functools.partial(out_grad_kernel, weight_scale),
        [shape((9 * state_chans, chans), F32)],
        [state, grad],
        "vvv",
        scratch=[pltpu.VMEM((3 * state_chans, 3 * chans), F32)],
        flops=each * narrow_rows,
    )
    local, lead = call(
        back_kernel,
        [near_shape, shape((rows + 2, cols, state_chans), BF)],
        [near, first, second, flip(out_kernel), lam],
        "vvvvv" + "vv",
        scratch=halo_scratch,
        flops=each * narrow_rows // 3,
        aliases=((0, 0),),
    )
    back = from_later(lead, totals)
    blocks = sizes["tm"]
    full = 9 * chans + blocks * frames
    full += -full % 64 if full % 32 else 0
    adjoint, sent, kept = call(
        functools.partial(in_grad_kernel, weight_scale, decay_scale, blocks),
        [
            shape((frames, rows + 2, cols, state_chans), BF),
            shape((full, chans), BF),
            shape((full, chans), F32),
        ],
        [local, back, back_reach, lam, wide, state, carry, out_part, gain_part],
        "vvvvvvvvv" + "vvv",
        scratch=[
            pltpu.VMEM((3 * chans, 3 * state_chans), F32),
            pltpu.VMEM((full, chans), F32),
            pltpu.VMEM((frames, state_chans), F32),
        ],
        flops=each * narrow_rows,
    )
    (video_grad,) = call(
        video_grad_kernel,
        [shape(video.shape, BF)],
        [adjoint, grad, flip(in_kernel), gain],
        "vvvv" + "h",
        scratch=[
            held(video),
            pltpu.SemaphoreType.DMA((frames // group_of(frames, LAST_GROUP),)),
        ],
        flops=each * narrow_rows,
    )
    own, other = tree_sum(sent, kept)
    in_grad, out_grad, gain_grad, decay_grad = call(
        functools.partial(result_kernel, blocks),
        [
            shape((3, 3, chans, state_chans), F32),
            shape((3, 3, state_chans, chans), F32),
            shape((1, chans), F32),
            shape((frames, state_chans), F32),
        ],
        [own, other],
        "vv" + "vvvv",
    )
    return act[None], video_grad[None], in_grad, out_grad, gain_grad[0], decay_grad


def solution(mesh):
    placed = (
        P("dp", "tm", "rows", None, None),
        P("dp", "tm", "rows", None, None),
        P(),
        P(),
        P(),
        P("tm", None),
    )
    return jax.shard_map(
        on_device,
        mesh=mesh,
        in_specs=placed,
        out_specs=(
            P("dp", "tm", "rows", None, None),
            P("dp", "tm", "rows", None, None),
            P(),
            P(),
            P(),
            P("tm", None),
        ),
        check_vma=False,
    )
```

```python
import functools
import math

import jax
import jax.numpy as jnp
from jax import lax
from jax.experimental import pallas as pl
from jax.experimental.pallas import tpu as pltpu
from jax.sharding import PartitionSpec as P

BF = jnp.bfloat16
F32 = jnp.float32
VMEM_LIMIT = 24 * 1024 * 1024
LAYER_GROUP = 8
LAST_GROUP = 8
OUTER_GROUP = 16
NEAR_GROUP = 8
SCAN_GROUP = 4
GELU_A = math.sqrt(2.0 / math.pi)
GELU_B = 0.044715


PLACES = {"s": pltpu.SMEM, "v": pltpu.VMEM, "h": pltpu.HBM}


def call(body, outs, ins, places, scratch=(), flops=0, aliases=()):
    moved = sum(math.prod(a.shape) * a.dtype.itemsize for a in list(ins) + list(outs))
    specs = [pl.BlockSpec(memory_space=PLACES[p]) for p in places]
    ins = [
        pltpu.with_memory_space_constraint(a, pltpu.HBM) if p == "h" else a for a, p in zip(ins, places)
    ]
    outs = [pltpu.HBM(a.shape, a.dtype) if p == "h" else a for a, p in zip(outs, places[len(ins) :])]
    return pl.pallas_call(
        body,
        out_shape=outs,
        in_specs=specs[: len(ins)],
        out_specs=specs[len(ins) :],
        scratch_shapes=list(scratch),
        input_output_aliases=dict(aliases),
        compiler_params=pltpu.CompilerParams(vmem_limit_bytes=VMEM_LIMIT),
        cost_estimate=pl.CostEstimate(flops=flops, bytes_accessed=moved, transcendentals=0),
    )(*ins)


def piece_copy(source, target, sems, n, group):
    span = pl.ds(n * group, group)
    return pltpu.make_async_copy(source.at[span], target.at[span], sems.at[n])


def held(array):
    return pltpu.VMEM(array.shape, array.dtype)


def shape(dims, dtype):
    return jax.ShapeDtypeStruct(tuple(dims), dtype)


def columns(count, width, lanes):
    return lax.rem(lax.broadcasted_iota(jnp.int32, (count, lanes), 0), width)


def from_left(field, column):
    return jnp.where(column == 0, 0.0, pltpu.roll(field, 1, 0))


def from_right(field, column, width):
    return jnp.where(column == width - 1, 0.0, pltpu.roll(field, field.shape[0] - 1, 0))


def taps(field, first, rows):
    frames, _, cols, chans = field.shape
    return jnp.concatenate(
        [field[:, first + i : first + i + rows].reshape(frames * rows * cols, chans) for i in range(3)],
        axis=1,
    )


def conv(field, first, rows, weights):
    _, _, cols, _ = field.shape
    out = weights.shape[1] // 3
    wide = jnp.dot(taps(field, first, rows), weights, preferred_element_type=F32)
    column = columns(wide.shape[0], cols, out)
    return (
        wide[:, out : 2 * out]
        + from_left(wide[:, :out], column)
        + from_right(wide[:, 2 * out :], column, cols)
    )


def spread(grad, cols):
    column = columns(grad.shape[0], cols, grad.shape[1])
    return jnp.concatenate(
        [
            from_right(grad, column, cols).astype(BF),
            grad.astype(BF),
            from_left(grad, column).astype(BF),
        ],
        axis=1,
    )


def outer(left, right):
    return lax.dot_general(left, right, (((0,), (0,)), ((), ())), preferred_element_type=F32)


def group_of(frames, most):
    size = most
    while frames % size:
        size -= 1
    return size


def fill_halo(wide_ref, own_ref, first_ref, second_ref):
    rows, deep = own_ref.shape[1], first_ref.shape[1]
    odd = lax.rem(lax.axis_index("rows"), 2) == 1
    wide_ref[:, deep : deep + rows] = own_ref[...]
    wide_ref[:, pl.ds(jnp.where(odd, 0, rows + deep), deep)] = first_ref[...]
    wide_ref[:, pl.ds(jnp.where(odd, rows + deep, 0), deep)] = second_ref[...]


def inside(field, width):
    count = field.shape[0]
    upper = jnp.where(lax.axis_index("rows") > 0, field[:width], 0.0)
    lower = jnp.where(lax.axis_index("rows") < lax.axis_size("rows") - 1, field[count - width :], 0.0)
    return jnp.concatenate([upper, field[width : count - width], lower], axis=0)


def near_kernel(own_ref, kernel_ref, near_ref, wide_ref):
    frames, rows, cols, chans = own_ref.shape
    group = group_of(frames, NEAR_GROUP)
    none = jnp.zeros((group, 2, cols, chans), BF)

    def step(n, _):
        span = pl.ds(n * group, group)
        wide_ref[:, :2] = none
        wide_ref[:, 2 : 2 + rows] = own_ref[span]
        wide_ref[:, 2 + rows :] = none
        near = conv(wide_ref[...], 0, rows + 2, kernel_ref[...])
        near_ref[span] = near.reshape(group, rows + 2, cols, near.shape[1])
        return 0

    lax.fori_loop(0, frames // group, step, 0)


def near_back_kernel(own_ref, kernel_ref, act_ref, near_ref, act_out, wide_ref, sem):
    copy = pltpu.make_async_copy(act_ref, act_out, sem)
    copy.start()
    near_kernel(own_ref, kernel_ref, near_ref, wide_ref)
    copy.wait()


def halo_part(first_ref, second_ref, kernel_ref, upper_ref, lower_ref):
    frames, deep, cols, chans = first_ref.shape
    state_chans = kernel_ref.shape[1] // 3
    odd = lax.rem(lax.axis_index("rows"), 2) == 1

    def put(out_ref, left, right, weights):
        pair = jnp.concatenate([left, right], axis=3).reshape(frames * deep * cols, 2 * chans)
        wide = jnp.dot(pair, weights, preferred_element_type=F32)
        column = columns(wide.shape[0], cols, state_chans)
        out_ref[...] = (
            wide[:, state_chans : 2 * state_chans]
            + from_left(wide[:, :state_chans], column)
            + from_right(wide[:, 2 * state_chans :], column, cols)
        ).reshape(frames, deep, cols, state_chans)

    def both(above_ref, below_ref):
        none = jnp.zeros((frames, 1, cols, chans), BF)
        above, below = above_ref[...], below_ref[...]
        put(upper_ref, above, jnp.concatenate([above[:, 1:], none], axis=1), kernel_ref[: 2 * chans])
        put(lower_ref, jnp.concatenate([none, below[:, :1]], axis=1), below, kernel_ref[chans:])

    @pl.when(odd)
    def _():
        both(first_ref, second_ref)

    @pl.when(jnp.logical_not(odd))
    def _():
        both(second_ref, first_ref)


def whole_rows(near, upper, lower):
    count, cols, chans = near.shape
    field = jnp.concatenate([near[:2] + upper, near[2 : count - 2], near[count - 2 :] + lower], axis=0)
    return inside(field.reshape(count * cols, chans), cols)


def drive_kernel(
    near_ref, own_ref, first_ref, second_ref, kernel_ref, lam_ref,
    kept_ref, local_ref, end_ref, wide_ref, upper_ref, lower_ref, sem,
):
    frames, rows_two, cols, state_chans = near_ref.shape
    fill_halo(wide_ref, own_ref, first_ref, second_ref)
    keep = pltpu.make_async_copy(wide_ref, kept_ref, sem)
    keep.start()
    halo_part(first_ref, second_ref, kernel_ref, upper_ref, lower_ref)
    group = group_of(frames, SCAN_GROUP)

    def step(n, state):
        for k in range(group):
            t = n * group + k
            state = lam_ref[t] * state + whole_rows(near_ref[t], upper_ref[t], lower_ref[t])
            local_ref[t] = state.reshape(rows_two, cols, state_chans)
        return state

    last = lax.fori_loop(0, frames // group, step, jnp.zeros((rows_two * cols, state_chans), F32))
    end_ref[...] = last.reshape(rows_two, cols, state_chans).astype(BF)
    keep.wait()


def layer_kernel(
    local_ref, carry_ref, reach_ref, own_ref, cot_ref, kernel_ref, gain_ref,
    state_out, act_ref, grad_ref, gain_grad_ref,
    own_in, cot_in, state_ref, sems,
):
    frames, rows, cols, chans = own_ref.shape
    group = group_of(frames, LAYER_GROUP)
    many = group * rows * cols
    carry = earlier(carry_ref, slice(None))
    steps = frames // group

    def start(n, _):
        piece_copy(own_ref, own_in, sems.at[0], n, group).start()
        piece_copy(cot_ref, cot_in, sems.at[1], n, group).start()
        return 0

    lax.fori_loop(0, steps, start, 0)

    def step(n, total):
        base = n * group
        state = jnp.stack(
            [(local_ref[base + k] + reach_ref[base + k] * carry).astype(BF) for k in range(group)]
        )
        state_ref[pl.ds(base, group)] = state
        piece_copy(state_ref, state_out, sems.at[2], n, group).start()
        flow = conv(state, 0, rows, kernel_ref[...])
        piece_copy(own_ref, own_in, sems.at[0], n, group).wait()
        piece_copy(cot_ref, cot_in, sems.at[1], n, group).wait()
        own = own_in[pl.ds(base, group)].reshape(many, chans).astype(F32)
        pre = flow + gain_ref[...] * own
        square = pre * pre
        half = 0.5 + 0.5 * jnp.tanh(pre * (GELU_A + (GELU_A * GELU_B) * square))
        act = pre * half
        slope = half + act * (1.0 - half) * (2.0 * GELU_A + (6.0 * GELU_A * GELU_B) * square)
        grad = cot_in[pl.ds(base, group)].reshape(many, chans).astype(F32) * slope
        act_ref[pl.ds(base, group)] = act.astype(BF).reshape(group, rows, cols, chans)
        grad_ref[pl.ds(base, group)] = grad.astype(BF).reshape(group, rows, cols, chans)
        return total + jnp.sum((grad * own).reshape(many // 8, 8, chans), axis=0)

    total = lax.fori_loop(0, steps, step, jnp.zeros((8, chans), F32))
    gain_grad_ref[...] = jnp.sum(total, axis=0, keepdims=True)

    def finish(n, _):
        piece_copy(state_ref, state_out, sems.at[2], n, group).wait()
        return 0

    lax.fori_loop(0, steps, finish, 0)


def put_blocks(total_ref, out_ref, scale):
    left, right = total_ref.shape[0] // 3, total_ref.shape[1] // 3
    for i in range(3):
        for j in range(3):
            at = (3 * i + j) * left
            out_ref[at : at + left] = (
                total_ref[i * left : (i + 1) * left, j * right : (j + 1) * right] * scale
            )


def out_grad_kernel(scale, state_ref, grad_ref, out_ref, total_ref):
    frames, rows, cols, chans = grad_ref.shape
    group = group_of(frames, 16)
    total_ref[...] = jnp.zeros_like(total_ref)

    def step(n, _):
        base = n * group
        grad = grad_ref[pl.ds(base, group)].reshape(group * rows * cols, chans).astype(F32)
        left = taps(state_ref[pl.ds(base, group)], 0, rows)
        total_ref[...] += outer(left, spread(grad, cols))
        return 0

    lax.fori_loop(0, frames // group, step, 0)
    put_blocks(total_ref, out_ref, scale)


def back_kernel(
    near_ref, first_ref, second_ref, kernel_ref, lam_ref,
    local_ref, lead_ref, upper_ref, lower_ref,
):
    frames, rows_two, cols, state_chans = near_ref.shape
    halo_part(first_ref, second_ref, kernel_ref, upper_ref, lower_ref)
    group = group_of(frames, SCAN_GROUP)

    def step(n, carry):
        for k in range(group):
            t = frames - 1 - (n * group + k)
            adjoint = whole_rows(near_ref[t], upper_ref[t], lower_ref[t]) + carry
            local_ref[t] = adjoint.reshape(rows_two, cols, state_chans)
            carry = lam_ref[t] * adjoint
        return carry

    lead = lax.fori_loop(0, frames // group, step, jnp.zeros((rows_two * cols, state_chans), F32))
    lead_ref[...] = lead.reshape(rows_two, cols, state_chans).astype(BF)


def in_grad_kernel(
    scale, decay_scale, blocks, local_ref, back_ref, reach_ref, lam_ref, wide_ref, state_ref,
    carry_ref, other_ref, gain_ref,
    adjoint_ref, sent_ref, kept_ref, total_ref, mine_ref, decay_ref,
):
    frames, rows_two, cols, chans = local_ref.shape
    rows = rows_two - 2
    group = group_of(frames, OUTER_GROUP)
    many = rows * cols
    back = later(back_ref, slice(None))
    alone = group == frames

    def step(n, previous):
        base = n * group
        kept = []
        for k in range(group):
            adjoint = local_ref[base + k] + reach_ref[base + k] * back
            adjoint_ref[base + k] = adjoint.astype(BF)
            mine = adjoint[1 : 1 + rows].reshape(many, chans)
            kept.append(mine)
            part = jnp.sum((mine * previous).reshape(many // 8, 8, chans), axis=0)
            decay_ref[pl.ds(base + k, 1)] = (
                jnp.sum(part, axis=0, keepdims=True) * lam_ref[base + k] * decay_scale
            )
            previous = state_ref[base + k, 1 : 1 + rows].reshape(many, chans).astype(F32)
        left = taps(wide_ref[pl.ds(base, group)], 1, rows)
        found = outer(left, spread(jnp.concatenate(kept, axis=0), cols))
        total_ref[...] = found if alone else jnp.where(n == 0, found, total_ref[...] + found)
        return previous

    before = earlier(carry_ref, slice(1, 1 + rows)).reshape(many, chans)
    if alone:
        step(0, before)
    else:
        lax.fori_loop(0, frames // group, step, before)
    count, full = other_ref.shape[0], mine_ref.shape[0]
    used = count + blocks * frames
    put_blocks(total_ref, mine_ref, scale)
    for n in range(blocks):
        mine_ref[count + n * frames : count + (n + 1) * frames] = jnp.where(
            lax.axis_index("tm") == n, decay_ref[...], 0.0
        )
    if full > used:
        mine_ref[used:] = jnp.zeros((full - used, chans), F32)
    row = lax.broadcasted_iota(jnp.int32, (full - count, chans), 0)
    rest = jnp.where(row == 0, gain_ref[...] * scale, 0.0)

    @pl.when(lax.rem(lax.axis_index("dp"), 2) == 0)
    def _():
        kept_ref[...] = mine_ref[...]
        sent_ref[:count] = other_ref[...].astype(BF)
        sent_ref[count:] = rest.astype(BF)

    @pl.when(lax.rem(lax.axis_index("dp"), 2) != 0)
    def _():
        sent_ref[...] = mine_ref[...].astype(BF)
        kept_ref[:count] = other_ref[...]
        kept_ref[count:] = rest


def result_kernel(blocks, mine, *refs):
    half_ref = refs[0]
    in_out, out_out, gain_out, decay_out, in_ref, out_ref, gain_ref, decay_ref, sems = refs[-9:]
    frames, chans = decay_ref.shape
    size = in_ref.shape[2]
    count = 9 * size
    first = lax.rem(lax.axis_index("dp"), 2) == (0 if mine else 1)

    def send(wide_ref, wide_out, small_ref, small_out):
        small = pltpu.make_async_copy(small_ref, small_out, sems.at[3])
        small.start()
        copies = []
        for i in range(3):
            for j in range(3):
                at = (3 * i + j) * size
                wide_ref[i, j] = half_ref[at : at + size].astype(F32)
            copies.append(pltpu.make_async_copy(wide_ref.at[i], wide_out.at[i], sems.at[i]))
            copies[-1].start()
        for copy in copies:
            copy.wait()
        small.wait()

    @pl.when(first)
    def _():
        decay = jnp.zeros((frames, chans), F32)
        for n in range(blocks):
            slot = half_ref[count + n * frames : count + (n + 1) * frames].astype(F32)
            decay = jnp.where(lax.axis_index("tm") == n, slot, decay)
        decay_ref[...] = decay
        send(in_ref, in_out, decay_ref, decay_out)

    @pl.when(jnp.logical_not(first))
    def _():
        gain_ref[...] = half_ref[count : count + 16].astype(F32)[:1]
        send(out_ref, out_out, gain_ref, gain_out)


def video_grad_kernel(adjoint_ref, grad_ref, kernel_ref, gain_ref, video_out, out_ref, sems):
    frames, rows, cols, chans = grad_ref.shape
    group = group_of(frames, LAST_GROUP)

    def step(n, _):
        base = n * group
        grad = grad_ref[pl.ds(base, group)].reshape(group * rows * cols, chans).astype(F32)
        flow = conv(adjoint_ref[pl.ds(base, group)], 0, rows, kernel_ref[...])
        out_ref[pl.ds(base, group)] = (
            (flow + gain_ref[...] * grad).astype(BF).reshape(group, rows, cols, chans)
        )
        piece_copy(out_ref, video_out, sems, n, group).start()
        return 0

    def finish(n, _):
        piece_copy(out_ref, video_out, sems, n, group).wait()
        return 0

    lax.fori_loop(0, frames // group, step, 0)
    lax.fori_loop(0, frames // group, finish, 0)


def edge_kernel(field_ref, first_ref, second_ref, sems):
    deep = first_ref.shape[1]
    last = field_ref.shape[1] - deep
    odd = lax.rem(lax.axis_index("rows"), 2)
    one = pltpu.make_async_copy(field_ref.at[:, pl.ds((1 - odd) * last, deep)], first_ref, sems.at[0])
    two = pltpu.make_async_copy(field_ref.at[:, pl.ds(odd * last, deep)], second_ref, sems.at[1])
    one.start()
    two.start()
    one.wait()
    two.wait()


def halo_pair(field, deep, read=False):
    count = lax.axis_size("rows")
    odd = lax.rem(lax.axis_index("rows"), 2)
    rows = field.shape[1]
    swap = lambda low: [p for i in range(low, count - 1, 2) for p in ((i, i + 1), (i + 1, i))]
    pick = lambda flag: lax.dynamic_slice_in_dim(field, flag * (rows - deep), deep, axis=1)
    if read:
        edges = shape((field.shape[0], deep) + field.shape[2:], field.dtype)
        first, second = call(
            edge_kernel, [edges, edges], [field], "hvv", scratch=[pltpu.SemaphoreType.DMA((2,))]
        )
    else:
        first, second = pick(1 - odd), pick(odd)
    first = lax.ppermute(first, "rows", swap(0))
    second = lax.ppermute(second, "rows", swap(1))
    return first, second


def carried(value, totals, way):
    count = lax.axis_size("tm")
    block = lax.axis_index("tm")
    if count == 1:
        return jnp.zeros(value.shape, BF)
    send = lambda v, k: lax.ppermute(v, "tm", [(i, (i + way * k) % count) for i in range(count)])
    found = send(value, 1)
    if count == 2:
        return found
    reaches = lambda k: (block >= k) if way == 1 else (block + k < count)
    found = jnp.where(reaches(1), found.astype(F32), 0.0)
    between = jnp.zeros_like(totals)
    for k in range(2, count):
        between = between + send(totals, k - 1)
        weight = jnp.exp(jnp.minimum(between, 0.0))
        found = found + jnp.where(reaches(k), weight * send(value, k).astype(F32), 0.0)
    return found.astype(BF)


def earlier(carry_ref, rows):
    carry = carry_ref[rows].astype(F32)
    return jnp.where(lax.axis_index("tm") > 0, carry, 0.0)


def later(back_ref, rows):
    back = back_ref[rows].astype(F32)
    return jnp.where(lax.axis_index("tm") < lax.axis_size("tm") - 1, back, 0.0)


def tree_sum(sent, kept):
    axes = ("tm", "rows", "dp")
    bits, devices = [], 1
    for axis in reversed(axes):
        size = 1
        while size < lax.axis_size(axis):
            bits.append((axis, size, size * devices))
            size *= 2
        devices *= lax.axis_size(axis)
    halves = [b for b in bits if b[0] == "dp"][0]
    group = [b for b in bits if b[0] == "dp"][1:2] + [b for b in bits if b[0] == "tm"][:1]
    far = [b for b in bits if b != halves and b not in group]

    def swap(value, mask):
        return lax.ppermute(value, axes, [(i, i ^ mask) for i in range(devices)])

    def combined(k):
        return sum(mask for n, (_, _, mask) in enumerate(group) if (k >> n) & 1)

    spot = 0
    for n, (axis, mask, _) in enumerate(group):
        spot = spot + jnp.where((lax.axis_index(axis) & mask) != 0, 1 << n, 0)
    ways = 1 << len(group)
    size = kept.shape[0] // ways
    half = kept + swap(sent, halves[2]).astype(F32)
    chunk = lambda k: lax.dynamic_slice_in_dim(half, (spot ^ k) * size, size, axis=0)
    chunks = lax.optimization_barrier([chunk(0)] + [chunk(k).astype(BF) for k in range(1, ways)])
    found = [swap(chunks[k], combined(k)) for k in range(1, ways)]
    total = chunks[0]
    for piece in found:
        total = total + piece.astype(F32)
    total = total.astype(BF)
    for _, _, mask in far:
        total = (total.astype(F32) + swap(total, mask).astype(F32)).astype(BF)
    found = [total] + [swap(total, combined(k)) for k in range(1, ways)]
    own = jnp.zeros(sent.shape, BF)
    for k, piece in enumerate(found):
        own = lax.dynamic_update_slice_in_dim(own, piece, (spot ^ k) * size, axis=0)
    return own, swap(own, halves[2])


def on_device(video, cotangent, in_kernel, out_kernel, skip_gain, log_decay):
    seqs, frames, rows, cols, chans = video.shape
    state_chans = in_kernel.shape[3]
    sizes = {axis: lax.axis_size(axis) for axis in ("tm", "rows", "dp")}
    devices = sizes["tm"] * sizes["rows"] * sizes["dp"]
    for size in sizes.values():
        assert size & (size - 1) == 0
    assert seqs == 1 and rows >= 2 and sizes["dp"] >= 2 and chans == state_chans
    video, cotangent = video[0], cotangent[0]
    cum = jnp.cumsum(log_decay, axis=0)
    totals = cum[-1:]
    lam = jnp.exp(log_decay)[:, None, :]
    reach = jnp.exp(cum)[:, None, :]
    back_reach = jnp.exp(totals - cum)[:, None, :]
    gain = skip_gain[None, :]
    flat = lambda k: k.transpose(0, 2, 1, 3).reshape(3 * k.shape[2], 3 * k.shape[3])
    flip = lambda k: k[::-1, ::-1].transpose(0, 3, 1, 2).reshape(3 * k.shape[3], 3 * k.shape[2])
    wide_rows = frames * (rows + 2) * cols
    narrow_rows = frames * rows * cols
    each = 2 * 9 * chans * state_chans
    weight_scale = 1.0 / math.sqrt(devices * narrow_rows * seqs)
    decay_scale = 1.0 / math.sqrt(seqs * rows * cols * sizes["rows"] * sizes["dp"])

    first, second = halo_pair(video, 2, True)
    near_shape = shape((frames, rows + 2, cols, state_chans), F32)
    near_scratch = [pltpu.VMEM((group_of(frames, NEAR_GROUP), rows + 4, cols, chans), BF)]
    halo_scratch = [pltpu.VMEM((frames, 2, cols, state_chans), F32)] * 2
    (near,) = call(
        near_kernel, [near_shape], [video, flat(in_kernel)], "vvv",
        scratch=near_scratch, flops=each * wide_rows,
    )
    wide, local, end = call(
        drive_kernel,
        [
            shape((frames, rows + 4, cols, chans), BF),
            near_shape,
            shape((rows + 2, cols, state_chans), BF),
        ],
        [near, video, first, second, flat(in_kernel), lam],
        "vvvvvv" + "hvv",
        scratch=[
            pltpu.VMEM((frames, rows + 4, cols, chans), BF),
            *halo_scratch,
            pltpu.SemaphoreType.DMA(()),
        ],
        flops=each * narrow_rows // 3,
        aliases=((0, 1),),
    )
    carry = carried(end, totals, 1)
    state, act, grad, gain_part = call(
        layer_kernel,
        [
            shape((frames, rows + 2, cols, state_chans), BF),
            shape(video.shape, BF),
            shape(video.shape, BF),
            shape((1, chans), F32),
        ],
        [local, carry, reach, video, cotangent, flat(out_kernel), gain],
        "vvvhhvv" + "hvvv",
        scratch=[
            held(video),
            held(video),
            pltpu.VMEM((frames, rows + 2, cols, state_chans), BF),
            pltpu.SemaphoreType.DMA((3, frames // group_of(frames, LAYER_GROUP))),
        ],
        flops=each * narrow_rows,
    )
    first, second = halo_pair(grad, 2)
    near, act = call(
        near_back_kernel,
        [near_shape, shape(act.shape, BF)],
        [grad, flip(out_kernel), act],
        "vvv" + "vh",
        scratch=[*near_scratch, pltpu.SemaphoreType.DMA(())],
        flops=each * wide_rows,
    )
    (out_part,) = call(
        functools.partial(out_grad_kernel, weight_scale),
        [shape((9 * state_chans, chans), F32)],
        [state, grad],
        "vvv",
        scratch=[pltpu.VMEM((3 * state_chans, 3 * chans), F32)],
        flops=each * narrow_rows,
    )
    local, lead = call(
        back_kernel,
        [near_shape, shape((rows + 2, cols, state_chans), BF)],
        [near, first, second, flip(out_kernel), lam],
        "vvvvv" + "vv",
        scratch=halo_scratch,
        flops=each * narrow_rows // 3,
        aliases=((0, 0),),
    )
    back = carried(lead, totals, -1)
    blocks = sizes["tm"]
    full = 9 * chans + blocks * frames
    full += -full % 64 if full % 32 else 0
    adjoint, sent, kept = call(
        functools.partial(in_grad_kernel, weight_scale, decay_scale, blocks),
        [
            shape((frames, rows + 2, cols, state_chans), BF),
            shape((full, chans), BF),
            shape((full, chans), F32),
        ],
        [local, back, back_reach, lam, wide, state, carry, out_part, gain_part],
        "vvvvvvvvv" + "vvv",
        scratch=[
            pltpu.VMEM((3 * chans, 3 * state_chans), F32),
            pltpu.VMEM((full, chans), F32),
            pltpu.VMEM((frames, state_chans), F32),
        ],
        flops=each * narrow_rows,
    )
    (video_grad,) = call(
        video_grad_kernel,
        [shape(video.shape, BF)],
        [adjoint, grad, flip(in_kernel), gain],
        "vvvv" + "h",
        scratch=[
            held(video),
            pltpu.SemaphoreType.DMA((frames // group_of(frames, LAST_GROUP),)),
        ],
        flops=each * narrow_rows,
    )
    own, other = tree_sum(sent, kept)
    results = [
        shape((3, 3, chans, state_chans), F32),
        shape((3, 3, state_chans, chans), F32),
        shape((1, chans), F32),
        shape((frames, state_chans), F32),
    ]
    scratch = [*[held(r) for r in results], pltpu.SemaphoreType.DMA((4,))]
    results = call(
        functools.partial(result_kernel, blocks, True), results, [own], "v" + "hhhh", scratch=scratch
    )
    in_grad, out_grad, gain_grad, decay_grad = call(
        functools.partial(result_kernel, blocks, False),
        [shape(r.shape, F32) for r in results],
        [other, *results],
        "vhhhh" + "hhhh",
        scratch=scratch,
        aliases=((1, 0), (2, 1), (3, 2), (4, 3)),
    )
    return act[None], video_grad[None], in_grad, out_grad, gain_grad[0], decay_grad


def solution(mesh):
    placed = (
        P("dp", "tm", "rows", None, None),
        P("dp", "tm", "rows", None, None),
        P(),
        P(),
        P(),
        P("tm", None),
    )
    return jax.shard_map(
        on_device,
        mesh=mesh,
        in_specs=placed,
        out_specs=(
            P("dp", "tm", "rows", None, None),
            P("dp", "tm", "rows", None, None),
            P(),
            P(),
            P(),
            P("tm", None),
        ),
        check_vma=False,
    )
```

```python
import functools
import math

import jax
import jax.numpy as jnp
from jax import lax
from jax.experimental import pallas as pl
from jax.experimental.pallas import tpu as pltpu
from jax.sharding import PartitionSpec as P

BF = jnp.bfloat16
F32 = jnp.float32
VMEM_LIMIT = 24 * 1024 * 1024
LAYER_GROUP = 8
LAST_GROUP = 8
OUTER_GROUP = 16
NEAR_GROUP = 16
SCAN_GROUP = 8
GELU_A = math.sqrt(2.0 / math.pi)
GELU_B = 0.044715


PLACES = {"s": pltpu.SMEM, "v": pltpu.VMEM, "h": pltpu.HBM}


def call(body, outs, ins, places, scratch=(), flops=0, aliases=()):
    moved = sum(math.prod(a.shape) * a.dtype.itemsize for a in list(ins) + list(outs))
    specs = [pl.BlockSpec(memory_space=PLACES[p]) for p in places]
    ins = [
        pltpu.with_memory_space_constraint(a, pltpu.HBM) if p == "h" else a for a, p in zip(ins, places)
    ]
    outs = [pltpu.HBM(a.shape, a.dtype) if p == "h" else a for a, p in zip(outs, places[len(ins) :])]
    return pl.pallas_call(
        body,
        out_shape=outs,
        in_specs=specs[: len(ins)],
        out_specs=specs[len(ins) :],
        scratch_shapes=list(scratch),
        input_output_aliases=dict(aliases),
        compiler_params=pltpu.CompilerParams(vmem_limit_bytes=VMEM_LIMIT),
        cost_estimate=pl.CostEstimate(flops=flops, bytes_accessed=moved, transcendentals=0),
    )(*ins)


def piece_copy(source, target, sems, n, group):
    span = pl.ds(n * group, group)
    return pltpu.make_async_copy(source.at[span], target.at[span], sems.at[n])


def held(array):
    return pltpu.VMEM(array.shape, array.dtype)


def shape(dims, dtype):
    return jax.ShapeDtypeStruct(tuple(dims), dtype)


def columns(count, width, lanes):
    return lax.rem(lax.broadcasted_iota(jnp.int32, (count, lanes), 0), width)


def from_left(field, column):
    return jnp.where(column == 0, 0.0, pltpu.roll(field, 1, 0))


def from_right(field, column, width):
    return jnp.where(column == width - 1, 0.0, pltpu.roll(field, field.shape[0] - 1, 0))


def taps(field, first, rows):
    frames, _, cols, chans = field.shape
    return jnp.concatenate(
        [field[:, first + i : first + i + rows].reshape(frames * rows * cols, chans) for i in range(3)],
        axis=1,
    )


def conv(field, first, rows, weights):
    _, _, cols, _ = field.shape
    out = weights.shape[1] // 3
    wide = jnp.dot(taps(field, first, rows), weights, preferred_element_type=F32)
    column = columns(wide.shape[0], cols, out)
    return (
        wide[:, out : 2 * out]
        + from_left(wide[:, :out], column)
        + from_right(wide[:, 2 * out :], column, cols)
    )


def spread(grad, cols):
    column = columns(grad.shape[0], cols, grad.shape[1])
    return jnp.concatenate(
        [
            from_right(grad, column, cols).astype(BF),
            grad.astype(BF),
            from_left(grad, column).astype(BF),
        ],
        axis=1,
    )


def outer(left, right):
    return lax.dot_general(left, right, (((0,), (0,)), ((), ())), preferred_element_type=F32)


def group_of(frames, most):
    size = most
    while frames % size:
        size -= 1
    return size


def fill_halo(wide_ref, own_ref, first_ref, second_ref):
    rows, deep = own_ref.shape[1], first_ref.shape[1]
    odd = lax.rem(lax.axis_index("rows"), 2) == 1
    wide_ref[:, deep : deep + rows] = own_ref[...]
    wide_ref[:, pl.ds(jnp.where(odd, 0, rows + deep), deep)] = first_ref[...]
    wide_ref[:, pl.ds(jnp.where(odd, rows + deep, 0), deep)] = second_ref[...]


def inside(field, width):
    count = field.shape[0]
    upper = jnp.where(lax.axis_index("rows") > 0, field[:width], 0.0)
    lower = jnp.where(lax.axis_index("rows") < lax.axis_size("rows") - 1, field[count - width :], 0.0)
    return jnp.concatenate([upper, field[width : count - width], lower], axis=0)


def near_kernel(own_ref, kernel_ref, near_ref, wide_ref):
    frames, rows, cols, chans = own_ref.shape
    group = group_of(frames, NEAR_GROUP)
    none = jnp.zeros((group, 2, cols, chans), BF)

    def step(n, _):
        span = pl.ds(n * group, group)
        wide_ref[:, :2] = none
        wide_ref[:, 2 : 2 + rows] = own_ref[span]
        wide_ref[:, 2 + rows :] = none
        near = conv(wide_ref[...], 0, rows + 2, kernel_ref[...])
        near_ref[span] = near.reshape(group, rows + 2, cols, near.shape[1])
        return 0

    lax.fori_loop(0, frames // group, step, 0)


def near_back_kernel(own_ref, kernel_ref, act_ref, near_ref, act_out, wide_ref, sem):
    copy = pltpu.make_async_copy(act_ref, act_out, sem)
    copy.start()
    near_kernel(own_ref, kernel_ref, near_ref, wide_ref)
    copy.wait()


def halo_part(first_ref, second_ref, kernel_ref, upper_ref, lower_ref):
    frames, deep, cols, chans = first_ref.shape
    state_chans = kernel_ref.shape[1] // 3
    odd = lax.rem(lax.axis_index("rows"), 2) == 1

    def put(out_ref, left, right, weights):
        pair = jnp.concatenate([left, right], axis=3).reshape(frames * deep * cols, 2 * chans)
        wide = jnp.dot(pair, weights, preferred_element_type=F32)
        column = columns(wide.shape[0], cols, state_chans)
        out_ref[...] = (
            wide[:, state_chans : 2 * state_chans]
            + from_left(wide[:, :state_chans], column)
            + from_right(wide[:, 2 * state_chans :], column, cols)
        ).reshape(frames, deep, cols, state_chans)

    def both(above_ref, below_ref):
        none = jnp.zeros((frames, 1, cols, chans), BF)
        above, below = above_ref[...], below_ref[...]
        put(upper_ref, above, jnp.concatenate([above[:, 1:], none], axis=1), kernel_ref[: 2 * chans])
        put(lower_ref, jnp.concatenate([none, below[:, :1]], axis=1), below, kernel_ref[chans:])

    @pl.when(odd)
    def _():
        both(first_ref, second_ref)

    @pl.when(jnp.logical_not(odd))
    def _():
        both(second_ref, first_ref)


def whole_rows(near, upper, lower):
    count, cols, chans = near.shape
    field = jnp.concatenate([near[:2] + upper, near[2 : count - 2], near[count - 2 :] + lower], axis=0)
    return inside(field.reshape(count * cols, chans), cols)


def drive_kernel(
    near_ref, own_ref, first_ref, second_ref, kernel_ref, lam_ref,
    kept_ref, local_ref, end_ref, wide_ref, upper_ref, lower_ref, sem,
):
    frames, rows_two, cols, state_chans = near_ref.shape
    fill_halo(wide_ref, own_ref, first_ref, second_ref)
    keep = pltpu.make_async_copy(wide_ref, kept_ref, sem)
    keep.start()
    halo_part(first_ref, second_ref, kernel_ref, upper_ref, lower_ref)
    group = group_of(frames, SCAN_GROUP)

    def step(n, state):
        for k in range(group):
            t = n * group + k
            state = lam_ref[t] * state + whole_rows(near_ref[t], upper_ref[t], lower_ref[t])
            local_ref[t] = state.reshape(rows_two, cols, state_chans)
        return state

    last = lax.fori_loop(0, frames // group, step, jnp.zeros((rows_two * cols, state_chans), F32))
    end_ref[...] = last.reshape(rows_two, cols, state_chans).astype(BF)
    keep.wait()


def layer_kernel(
    local_ref, carry_ref, reach_ref, own_ref, cot_ref, kernel_ref, gain_ref,
    state_out, act_ref, grad_ref, gain_grad_ref,
    own_in, cot_in, state_ref, sems,
):
    frames, rows, cols, chans = own_ref.shape
    group = group_of(frames, LAYER_GROUP)
    many = group * rows * cols
    carry = earlier(carry_ref, slice(None))
    steps = frames // group

    def start(n, _):
        piece_copy(own_ref, own_in, sems.at[0], n, group).start()
        piece_copy(cot_ref, cot_in, sems.at[1], n, group).start()
        return 0

    lax.fori_loop(0, steps, start, 0)

    def step(n, total):
        base = n * group
        state = jnp.stack(
            [(local_ref[base + k] + reach_ref[base + k] * carry).astype(BF) for k in range(group)]
        )
        state_ref[pl.ds(base, group)] = state
        piece_copy(state_ref, state_out, sems.at[2], n, group).start()
        flow = conv(state, 0, rows, kernel_ref[...])
        piece_copy(own_ref, own_in, sems.at[0], n, group).wait()
        piece_copy(cot_ref, cot_in, sems.at[1], n, group).wait()
        own = own_in[pl.ds(base, group)].reshape(many, chans).astype(F32)
        pre = flow + gain_ref[...] * own
        square = pre * pre
        half = 0.5 + 0.5 * jnp.tanh(pre * (GELU_A + (GELU_A * GELU_B) * square))
        act = pre * half
        slope = half + act * (1.0 - half) * (2.0 * GELU_A + (6.0 * GELU_A * GELU_B) * square)
        grad = cot_in[pl.ds(base, group)].reshape(many, chans).astype(F32) * slope
        act_ref[pl.ds(base, group)] = act.astype(BF).reshape(group, rows, cols, chans)
        grad_ref[pl.ds(base, group)] = grad.astype(BF).reshape(group, rows, cols, chans)
        return total + jnp.sum((grad * own).reshape(many // 8, 8, chans), axis=0)

    total = lax.fori_loop(0, steps, step, jnp.zeros((8, chans), F32))
    gain_grad_ref[...] = jnp.sum(total, axis=0, keepdims=True)

    def finish(n, _):
        piece_copy(state_ref, state_out, sems.at[2], n, group).wait()
        return 0

    lax.fori_loop(0, steps, finish, 0)


def put_blocks(total_ref, out_ref, scale):
    left, right = total_ref.shape[0] // 3, total_ref.shape[1] // 3
    for i in range(3):
        for j in range(3):
            at = (3 * i + j) * left
            out_ref[at : at + left] = (
                total_ref[i * left : (i + 1) * left, j * right : (j + 1) * right] * scale
            )


def out_grad_kernel(scale, state_ref, grad_ref, out_ref, total_ref):
    frames, rows, cols, chans = grad_ref.shape
    group = group_of(frames, 16)
    total_ref[...] = jnp.zeros_like(total_ref)

    def step(n, _):
        base = n * group
        grad = grad_ref[pl.ds(base, group)].reshape(group * rows * cols, chans).astype(F32)
        left = taps(state_ref[pl.ds(base, group)], 0, rows)
        total_ref[...] += outer(left, spread(grad, cols))
        return 0

    lax.fori_loop(0, frames // group, step, 0)
    put_blocks(total_ref, out_ref, scale)


def back_kernel(
    near_ref, first_ref, second_ref, kernel_ref, lam_ref,
    local_ref, lead_ref, upper_ref, lower_ref,
):
    frames, rows_two, cols, state_chans = near_ref.shape
    halo_part(first_ref, second_ref, kernel_ref, upper_ref, lower_ref)
    group = group_of(frames, SCAN_GROUP)

    def step(n, carry):
        for k in range(group):
            t = frames - 1 - (n * group + k)
            adjoint = whole_rows(near_ref[t], upper_ref[t], lower_ref[t]) + carry
            local_ref[t] = adjoint.reshape(rows_two, cols, state_chans)
            carry = lam_ref[t] * adjoint
        return carry

    lead = lax.fori_loop(0, frames // group, step, jnp.zeros((rows_two * cols, state_chans), F32))
    lead_ref[...] = lead.reshape(rows_two, cols, state_chans).astype(BF)


def in_grad_kernel(
    scale, decay_scale, blocks, local_ref, back_ref, reach_ref, lam_ref, wide_ref, state_ref,
    carry_ref, other_ref, gain_ref,
    adjoint_ref, sent_ref, kept_ref, total_ref, mine_ref, decay_ref,
):
    frames, rows_two, cols, chans = local_ref.shape
    rows = rows_two - 2
    group = group_of(frames, OUTER_GROUP)
    many = rows * cols
    back = later(back_ref, slice(None))
    alone = group == frames

    def step(n, previous):
        base = n * group
        kept = []
        for k in range(group):
            adjoint = local_ref[base + k] + reach_ref[base + k] * back
            adjoint_ref[base + k] = adjoint.astype(BF)
            mine = adjoint[1 : 1 + rows].reshape(many, chans)
            kept.append(mine)
            part = jnp.sum((mine * previous).reshape(many // 8, 8, chans), axis=0)
            decay_ref[pl.ds(base + k, 1)] = (
                jnp.sum(part, axis=0, keepdims=True) * lam_ref[base + k] * decay_scale
            )
            previous = state_ref[base + k, 1 : 1 + rows].reshape(many, chans).astype(F32)
        left = taps(wide_ref[pl.ds(base, group)], 1, rows)
        found = outer(left, spread(jnp.concatenate(kept, axis=0), cols))
        total_ref[...] = found if alone else jnp.where(n == 0, found, total_ref[...] + found)
        return previous

    before = earlier(carry_ref, slice(1, 1 + rows)).reshape(many, chans)
    if alone:
        step(0, before)
    else:
        lax.fori_loop(0, frames // group, step, before)
    count, full = other_ref.shape[0], mine_ref.shape[0]
    used = count + blocks * frames
    put_blocks(total_ref, mine_ref, scale)
    for n in range(blocks):
        mine_ref[count + n * frames : count + (n + 1) * frames] = jnp.where(
            lax.axis_index("tm") == n, decay_ref[...], 0.0
        )
    if full > used:
        mine_ref[used:] = jnp.zeros((full - used, chans), F32)
    row = lax.broadcasted_iota(jnp.int32, (full - count, chans), 0)
    rest = jnp.where(row == 0, gain_ref[...] * scale, 0.0)

    @pl.when(lax.rem(lax.axis_index("dp"), 2) == 0)
    def _():
        kept_ref[...] = mine_ref[...]
        sent_ref[:count] = other_ref[...].astype(BF)
        sent_ref[count:] = rest.astype(BF)

    @pl.when(lax.rem(lax.axis_index("dp"), 2) != 0)
    def _():
        sent_ref[...] = mine_ref[...].astype(BF)
        kept_ref[:count] = other_ref[...]
        kept_ref[count:] = rest


def result_kernel(blocks, mine, *refs):
    half_ref = refs[0]
    in_out, out_out, gain_out, decay_out, in_ref, out_ref, gain_ref, decay_ref, sems = refs[-9:]
    frames, chans = decay_ref.shape
    size = in_ref.shape[2]
    count = 9 * size
    first = lax.rem(lax.axis_index("dp"), 2) == (0 if mine else 1)

    def send(wide_ref, wide_out, small_ref, small_out):
        small = pltpu.make_async_copy(small_ref, small_out, sems.at[3])
        small.start()
        copies = []
        for i in range(3):
            for j in range(3):
                at = (3 * i + j) * size
                wide_ref[i, j] = half_ref[at : at + size].astype(F32)
            copies.append(pltpu.make_async_copy(wide_ref.at[i], wide_out.at[i], sems.at[i]))
            copies[-1].start()
        for copy in copies:
            copy.wait()
        small.wait()

    @pl.when(first)
    def _():
        decay = jnp.zeros((frames, chans), F32)
        for n in range(blocks):
            slot = half_ref[count + n * frames : count + (n + 1) * frames].astype(F32)
            decay = jnp.where(lax.axis_index("tm") == n, slot, decay)
        decay_ref[...] = decay
        send(in_ref, in_out, decay_ref, decay_out)

    @pl.when(jnp.logical_not(first))
    def _():
        gain_ref[...] = half_ref[count : count + 16].astype(F32)[:1]
        send(out_ref, out_out, gain_ref, gain_out)


def video_grad_kernel(adjoint_ref, grad_ref, kernel_ref, gain_ref, video_out, out_ref, sems):
    frames, rows, cols, chans = grad_ref.shape
    group = group_of(frames, LAST_GROUP)

    def step(n, _):
        base = n * group
        grad = grad_ref[pl.ds(base, group)].reshape(group * rows * cols, chans).astype(F32)
        flow = conv(adjoint_ref[pl.ds(base, group)], 0, rows, kernel_ref[...])
        out_ref[pl.ds(base, group)] = (
            (flow + gain_ref[...] * grad).astype(BF).reshape(group, rows, cols, chans)
        )
        piece_copy(out_ref, video_out, sems, n, group).start()
        return 0

    def finish(n, _):
        piece_copy(out_ref, video_out, sems, n, group).wait()
        return 0

    lax.fori_loop(0, frames // group, step, 0)
    lax.fori_loop(0, frames // group, finish, 0)


def edge_kernel(field_ref, first_ref, second_ref, sems):
    deep = first_ref.shape[1]
    last = field_ref.shape[1] - deep
    odd = lax.rem(lax.axis_index("rows"), 2)
    one = pltpu.make_async_copy(field_ref.at[:, pl.ds((1 - odd) * last, deep)], first_ref, sems.at[0])
    two = pltpu.make_async_copy(field_ref.at[:, pl.ds(odd * last, deep)], second_ref, sems.at[1])
    one.start()
    two.start()
    one.wait()
    two.wait()


def halo_pair(field, deep, read=False):
    count = lax.axis_size("rows")
    odd = lax.rem(lax.axis_index("rows"), 2)
    rows = field.shape[1]
    swap = lambda low: [p for i in range(low, count - 1, 2) for p in ((i, i + 1), (i + 1, i))]
    pick = lambda flag: lax.dynamic_slice_in_dim(field, flag * (rows - deep), deep, axis=1)
    if read:
        edges = shape((field.shape[0], deep) + field.shape[2:], field.dtype)
        first, second = call(
            edge_kernel, [edges, edges], [field], "hvv", scratch=[pltpu.SemaphoreType.DMA((2,))]
        )
    else:
        first, second = pick(1 - odd), pick(odd)
    first = lax.ppermute(first, "rows", swap(0))
    second = lax.ppermute(second, "rows", swap(1))
    return first, second


def carried(value, totals, way):
    count = lax.axis_size("tm")
    block = lax.axis_index("tm")
    if count == 1:
        return jnp.zeros(value.shape, BF)
    send = lambda v, k: lax.ppermute(v, "tm", [(i, (i + way * k) % count) for i in range(count)])
    found = send(value, 1)
    if count == 2:
        return found
    reaches = lambda k: (block >= k) if way == 1 else (block + k < count)
    found = jnp.where(reaches(1), found.astype(F32), 0.0)
    between = jnp.zeros_like(totals)
    for k in range(2, count):
        between = between + send(totals, k - 1)
        weight = jnp.exp(jnp.minimum(between, 0.0))
        found = found + jnp.where(reaches(k), weight * send(value, k).astype(F32), 0.0)
    return found.astype(BF)


def earlier(carry_ref, rows):
    carry = carry_ref[rows].astype(F32)
    return jnp.where(lax.axis_index("tm") > 0, carry, 0.0)


def later(back_ref, rows):
    back = back_ref[rows].astype(F32)
    return jnp.where(lax.axis_index("tm") < lax.axis_size("tm") - 1, back, 0.0)


def tree_sum(sent, kept):
    axes = ("tm", "rows", "dp")
    bits, devices = [], 1
    for axis in reversed(axes):
        size = 1
        while size < lax.axis_size(axis):
            bits.append((axis, size, size * devices))
            size *= 2
        devices *= lax.axis_size(axis)
    halves = [b for b in bits if b[0] == "dp"][0]
    group = [b for b in bits if b[0] == "dp"][1:2] + [b for b in bits if b[0] == "tm"][:1]
    far = [b for b in bits if b != halves and b not in group]

    def swap(value, mask):
        return lax.ppermute(value, axes, [(i, i ^ mask) for i in range(devices)])

    def combined(k):
        return sum(mask for n, (_, _, mask) in enumerate(group) if (k >> n) & 1)

    spot = 0
    for n, (axis, mask, _) in enumerate(group):
        spot = spot + jnp.where((lax.axis_index(axis) & mask) != 0, 1 << n, 0)
    ways = 1 << len(group)
    size = kept.shape[0] // ways
    half = kept + swap(sent, halves[2]).astype(F32)
    chunk = lambda k: lax.dynamic_slice_in_dim(half, (spot ^ k) * size, size, axis=0)
    chunks = lax.optimization_barrier([chunk(0)] + [chunk(k).astype(BF) for k in range(1, ways)])
    found = [swap(chunks[k], combined(k)) for k in range(1, ways)]
    total = chunks[0]
    for piece in found:
        total = total + piece.astype(F32)
    total = total.astype(BF)
    while far:
        (_, _, one), *far = far
        if far:
            (_, _, two), *far = far
            swapped = [swap(total, m).astype(F32) for m in (one, two, one + two)]
            total = ((total.astype(F32) + swapped[0]) + (swapped[1] + swapped[2])).astype(BF)
        else:
            total = (total.astype(F32) + swap(total, one).astype(F32)).astype(BF)
    found = [total] + [swap(total, combined(k)) for k in range(1, ways)]
    own = jnp.zeros(sent.shape, BF)
    for k, piece in enumerate(found):
        own = lax.dynamic_update_slice_in_dim(own, piece, (spot ^ k) * size, axis=0)
    return own, swap(own, halves[2])


def on_device(video, cotangent, in_kernel, out_kernel, skip_gain, log_decay):
    seqs, frames, rows, cols, chans = video.shape
    state_chans = in_kernel.shape[3]
    sizes = {axis: lax.axis_size(axis) for axis in ("tm", "rows", "dp")}
    devices = sizes["tm"] * sizes["rows"] * sizes["dp"]
    for size in sizes.values():
        assert size & (size - 1) == 0
    assert seqs == 1 and rows >= 2 and sizes["dp"] >= 2 and chans == state_chans
    video, cotangent = video[0], cotangent[0]
    cum = jnp.cumsum(log_decay, axis=0)
    totals = cum[-1:]
    lam = jnp.exp(log_decay)[:, None, :]
    reach = jnp.exp(cum)[:, None, :]
    back_reach = jnp.exp(totals - cum)[:, None, :]
    gain = skip_gain[None, :]
    flat = lambda k: k.transpose(0, 2, 1, 3).reshape(3 * k.shape[2], 3 * k.shape[3])
    flip = lambda k: k[::-1, ::-1].transpose(0, 3, 1, 2).reshape(3 * k.shape[3], 3 * k.shape[2])
    wide_rows = frames * (rows + 2) * cols
    narrow_rows = frames * rows * cols
    each = 2 * 9 * chans * state_chans
    weight_scale = 1.0 / math.sqrt(devices * narrow_rows * seqs)
    decay_scale = 1.0 / math.sqrt(seqs * rows * cols * sizes["rows"] * sizes["dp"])

    first, second = halo_pair(video, 2, True)
    near_shape = shape((frames, rows + 2, cols, state_chans), F32)
    near_scratch = [pltpu.VMEM((group_of(frames, NEAR_GROUP), rows + 4, cols, chans), BF)]
    halo_scratch = [pltpu.VMEM((frames, 2, cols, state_chans), F32)] * 2
    (near,) = call(
        near_kernel, [near_shape], [video, flat(in_kernel)], "vvv",
        scratch=near_scratch, flops=each * wide_rows,
    )
    wide, local, end = call(
        drive_kernel,
        [
            shape((frames, rows + 4, cols, chans), BF),
            near_shape,
            shape((rows + 2, cols, state_chans), BF),
        ],
        [near, video, first, second, flat(in_kernel), lam],
        "vvvvvv" + "hvv",
        scratch=[
            pltpu.VMEM((frames, rows + 4, cols, chans), BF),
            *halo_scratch,
            pltpu.SemaphoreType.DMA(()),
        ],
        flops=each * narrow_rows // 3,
        aliases=((0, 1),),
    )
    carry = carried(end, totals, 1)
    state, act, grad, gain_part = call(
        layer_kernel,
        [
            shape((frames, rows + 2, cols, state_chans), BF),
            shape(video.shape, BF),
            shape(video.shape, BF),
            shape((1, chans), F32),
        ],
        [local, carry, reach, video, cotangent, flat(out_kernel), gain],
        "vvvhhvv" + "hvvv",
        scratch=[
            held(video),
            held(video),
            pltpu.VMEM((frames, rows + 2, cols, state_chans), BF),
            pltpu.SemaphoreType.DMA((3, frames // group_of(frames, LAYER_GROUP))),
        ],
        flops=each * narrow_rows,
    )
    first, second = halo_pair(grad, 2)
    near, act = call(
        near_back_kernel,
        [near_shape, shape(act.shape, BF)],
        [grad, flip(out_kernel), act],
        "vvv" + "vh",
        scratch=[*near_scratch, pltpu.SemaphoreType.DMA(())],
        flops=each * wide_rows,
    )
    (out_part,) = call(
        functools.partial(out_grad_kernel, weight_scale),
        [shape((9 * state_chans, chans), F32)],
        [state, grad],
        "vvv",
        scratch=[pltpu.VMEM((3 * state_chans, 3 * chans), F32)],
        flops=each * narrow_rows,
    )
    local, lead = call(
        back_kernel,
        [near_shape, shape((rows + 2, cols, state_chans), BF)],
        [near, first, second, flip(out_kernel), lam],
        "vvvvv" + "vv",
        scratch=halo_scratch,
        flops=each * narrow_rows // 3,
        aliases=((0, 0),),
    )
    back = carried(lead, totals, -1)
    blocks = sizes["tm"]
    full = 9 * chans + blocks * frames
    full += -full % 64 if full % 32 else 0
    adjoint, sent, kept = call(
        functools.partial(in_grad_kernel, weight_scale, decay_scale, blocks),
        [
            shape((frames, rows + 2, cols, state_chans), BF),
            shape((full, chans), BF),
            shape((full, chans), F32),
        ],
        [local, back, back_reach, lam, wide, state, carry, out_part, gain_part],
        "vvvvvvvvv" + "vvv",
        scratch=[
            pltpu.VMEM((3 * chans, 3 * state_chans), F32),
            pltpu.VMEM((full, chans), F32),
            pltpu.VMEM((frames, state_chans), F32),
        ],
        flops=each * narrow_rows,
    )
    (video_grad,) = call(
        video_grad_kernel,
        [shape(video.shape, BF)],
        [adjoint, grad, flip(in_kernel), gain],
        "vvvv" + "h",
        scratch=[
            held(video),
            pltpu.SemaphoreType.DMA((frames // group_of(frames, LAST_GROUP),)),
        ],
        flops=each * narrow_rows,
    )
    own, other = tree_sum(sent, kept)
    results = [
        shape((3, 3, chans, state_chans), F32),
        shape((3, 3, state_chans, chans), F32),
        shape((1, chans), F32),
        shape((frames, state_chans), F32),
    ]
    scratch = [*[held(r) for r in results], pltpu.SemaphoreType.DMA((4,))]
    results = call(
        functools.partial(result_kernel, blocks, True), results, [own], "v" + "hhhh", scratch=scratch
    )
    in_grad, out_grad, gain_grad, decay_grad = call(
        functools.partial(result_kernel, blocks, False),
        [shape(r.shape, F32) for r in results],
        [other, *results],
        "vhhhh" + "hhhh",
        scratch=scratch,
        aliases=((1, 0), (2, 1), (3, 2), (4, 3)),
    )
    return act[None], video_grad[None], in_grad, out_grad, gain_grad[0], decay_grad


def solution(mesh):
    placed = (
        P("dp", "tm", "rows", None, None),
        P("dp", "tm", "rows", None, None),
        P(),
        P(),
        P(),
        P("tm", None),
    )
    return jax.shard_map(
        on_device,
        mesh=mesh,
        in_specs=placed,
        out_specs=(
            P("dp", "tm", "rows", None, None),
            P("dp", "tm", "rows", None, None),
            P(),
            P(),
            P(),
            P("tm", None),
        ),
        check_vma=False,
    )
```
